32 devices in a mesh: set: 4 (over z), path: 2 (over y), tm: 4 (over x, core).
Axes of the slice: x: 2, y: 2, z: 4, core: 2. Of those that a mesh axis runs over, the one named last changes fastest.
Arguments:
- normals: bfloat16 [1024, 2048], P(('set', 'path'), 'tm'), parts along dimension 0, may hold values from -6 to 6
- orth_normals: bfloat16 [1024, 2048], P(('set', 'path'), 'tm'), parts along dimension 0, may hold values from -6 to 6
- forward_var: float32 [8192], P(('set', 'tm')), parts along dimension 0, may hold values from 0.02 to 0.2
- hurst: float32 [4], P('set'), parts along dimension 0, may hold values from 0.05 to 0.25
- eta: float32 [4], P('set'), parts along dimension 0, may hold values from 1 to 2.5
- rho: float32 [4], P('set'), parts along dimension 0, may hold values from -0.95 to -0.5
- strike_index: int32 [1024], P('set'), parts along dimension 0, may hold values from 0 to 10
- maturity_index: int32 [1024], P('set'), parts along dimension 0, may hold values from 0 to 2047
Outputs:
- log_price: float32 [1024, 2048], P(('set', 'path'), 'tm'), parts along dimension 0
- prices: float32 [1024], P('set'), parts along dimension 0
The draws below stay inside these ranges and needn't reach their ends.
There are 4 independent parts, one for each index of `set`. The reference program is written for one: setup_inputs(seed, part) draws one part's arguments, and reference() takes and returns one part's arrays. A program takes and returns all parts, laid end to end along the dimension named above; each array names one. Nothing has to cross between parts.
All inputs are finite; a program needn't handle non-finite values.
Results may differ from the reference program's by a relative error of at most 0.0047.
The reference program's roundings to bfloat16 on the way count: a program that leaves them out, or rounds other values in their place, can miss the bound.
Values may be sent and summed in bfloat16 or wider, within the bound.
No kernel may reach another device: no remote copies, remote signals or barrier semaphores. Data moves between devices by JAX's collectives and lax.ppermute only.
A program may use at most 64 MiB of HBM per device.

```python
import math
import jax
import jax.numpy as jnp
from jax import lax

STEPS = 2048
QUOTES = 256
STRIKES = 11
PATHS = 256


def set_ends(drawn, key, least, high):
    place = [jax.random.randint(jax.random.fold_in(key, axis), (), 0, length) for axis, length in enumerate(drawn.shape)]
    main_axis = drawn.shape.index(max(drawn.shape))
    next_to = place[:main_axis] + [(place[main_axis] + 1) % drawn.shape[main_axis]] + place[main_axis + 1:]
    return drawn.at[tuple(place)].set(least).at[tuple(next_to)].set(high)


def steps_of(rng, dims, pieces, least, high):
    def one(dim, blocks):
        draws = jax.random.uniform(jax.random.fold_in(jax.random.fold_in(rng, 6), dim), (blocks,), jnp.float32, least / len(pieces), high / len(pieces))
        return jnp.repeat(jnp.exp(draws), dims[dim] // blocks).reshape((-1,) + (1,) * (len(dims) - dim - 1))

    loudness = one(*pieces[0])
    for cut in pieces[1:]:
        loudness = loudness * one(*cut)
    return loudness


def scatter_about(key, extent, scale, most, cuts=(), held_as=jnp.bfloat16):
    loudness = steps_of(key, extent, cuts, -0.22, 0.18) if cuts else 1.0
    drawn = jax.random.normal(key, extent, jnp.float32) * scale * loudness
    return jnp.minimum(jnp.maximum(drawn, -most), most).astype(held_as)


def setup_inputs(seed: int = 0, part: int = 0) -> dict:
    keys = jax.random.split(jax.random.key(seed), 9)
    own_keys = jax.random.split(jax.random.fold_in(keys[8], part), 9)
    return {
        "normals": scatter_about(own_keys[0], (PATHS, STEPS), 1.0, 6.0, ((0, 2), (1, 4))),
        "orth_normals": scatter_about(own_keys[1], (PATHS, STEPS), 1.0, 6.0, ((0, 2), (1, 4))),
        "forward_var": jnp.clip(jnp.exp(math.log(0.2) - 2.3025851 * jax.random.uniform(own_keys[2], (STEPS,), jnp.float32) ** steps_of(own_keys[2], (STEPS,), ((0, 4),), -0.2, 0.2)), 0.02, 0.2),
        "hurst": jnp.clip(jax.random.uniform(own_keys[3], (1,), jnp.float32, 0.05, 0.25), 0.05, 0.25),
        "eta": jnp.clip(jax.random.uniform(own_keys[4], (1,), jnp.float32, 1.0, 2.5), 1.0, 2.5),
        "rho": jnp.clip(jax.random.uniform(own_keys[5], (1,), jnp.float32, -0.95, -0.5), -0.95, -0.5),
        "strike_index": set_ends(jax.random.randint(own_keys[6], (QUOTES,), 0, STRIKES), jax.random.fold_in(own_keys[6], 1), 0, STRIKES - 1).astype(jnp.int32),
        "maturity_index": set_ends(jax.random.randint(own_keys[7], (QUOTES,), 0, STEPS), jax.random.fold_in(own_keys[7], 1), 0, STEPS - 1).astype(jnp.int32),
    }


horizon = 2.0

def increment_block(row_start, row_count, col_start, col_count, steps):
    rows = row_start + jnp.arange(row_count, dtype=jnp.int32)
    cols = col_start + jnp.arange(col_count, dtype=jnp.int32)
    period = 4 * (2 * steps + 1)
    phase = (2 * rows[:, None] + 1) * (2 * cols[None, :] + 1) % period
    step = horizon / steps
    scale = math.sqrt(step) * 2.0 / math.sqrt(2 * steps + 1)
    return (scale * jnp.cos(math.pi * phase.astype(jnp.float32) / (2 * (2 * steps + 1)))).astype(jnp.bfloat16)

def kernel_block(hurst_value, step, lag):
    expo = hurst_value - 0.5
    safe = jnp.maximum(lag, 1).astype(jnp.float32)
    inner = -jnp.expm1((expo + 1.0) * jnp.log1p(-1.0 / safe))
    log_b = ((expo + 1.0) * jnp.log(safe) + jnp.log(inner) - jnp.log(expo + 1.0)) / expo
    values = jnp.sqrt(2.0 * hurst_value) * jnp.exp(expo * (log_b + math.log(step)))
    return jnp.where(lag >= 1, values, 0.0).astype(jnp.bfloat16)

def reference(normals, orth_normals, forward_var, hurst, eta, rho, strike_index, maturity_index):
    steps = normals.shape[1]
    step = horizon / steps
    table = increment_block(0, steps, 0, steps, steps)
    dw = jnp.dot(normals, table, preferred_element_type=jnp.float32).astype(jnp.bfloat16)
    ar = jnp.arange(steps, dtype=jnp.int32)
    lag = ar[None, :] - ar[:, None]
    volterra = jnp.dot(dw, kernel_block(hurst[0], step, lag), preferred_element_type=jnp.float32)
    times = ar.astype(jnp.float32) * step
    variance = forward_var[None, :] * jnp.exp(eta[0] * volterra - 0.5 * eta[0] * eta[0] * (times ** (2.0 * hurst[0]))[None, :])
    noise = rho[0] * dw.astype(jnp.float32) + jnp.sqrt(1.0 - rho[0] * rho[0]) * math.sqrt(step) * orth_normals.astype(jnp.float32)
    increment = jnp.sqrt(variance) * noise - 0.5 * variance * step
    log_price = jnp.cumsum(increment, axis=1)
    spot = jnp.exp(jnp.take(log_price, maturity_index, axis=1))
    strikes = 0.5 + strike_index.astype(jnp.float32) / (STRIKES - 1)
    prices = lax.optimization_barrier(jnp.sum(jnp.maximum(spot - strikes[None, :], 0.0), axis=0)) / normals.shape[0]
    return (log_price, prices)
```

```python
import functools
import math

import jax
import jax.numpy as jnp
import numpy as np
from jax import lax
from jax.experimental import pallas as pl
from jax.experimental.pallas import tpu as pltpu
from jax.sharding import PartitionSpec as P

STRIKES = 11
HORIZON = 2.0
LANES = 128
BLOCK = 256
FINE = 64


def base_angles(steps):
    period = 4 * (2 * steps + 1)
    fine = 2 * np.arange(FINE) + 1
    coarse = 2 * FINE * np.arange(steps // FINE)
    lane = 2 * np.arange(LANES) + 1
    strip = 2 * LANES * np.arange(LANES)
    rows = []
    for left in (fine, coarse):
        for right in (strip, lane):
            turns = (left[:, None] * right[None, :]) % period
            angle = np.pi * turns / (2 * (2 * steps + 1))
            rows += [np.cos(angle), np.sin(angle)]
    return np.concatenate(rows, axis=0).astype(np.float32)


def prepare(steps, base_ref, g_ref, maturity_ref, table_ref, toeplitz_ref, mask_ref, fine_cos, fine_sin, coarse_cos, coarse_sin):
    coarse = steps // FINE
    strips = steps // LANES
    step = HORIZON / steps
    scale = math.sqrt(step) * 2.0 / math.sqrt(2 * steps + 1)

    at = 0
    for count, cos_ref, sin_ref, factor in ((FINE, fine_cos, fine_sin, None), (coarse, coarse_cos, coarse_sin, scale)):
        c1, s1, c2, s2 = (base_ref[at + n * count : at + (n + 1) * count, :] for n in range(4))
        at += 4 * count
        if factor is not None:
            c2, s2 = c2 * factor, s2 * factor
        for v in range(strips):
            cv = jnp.broadcast_to(c1[:, v : v + 1], (count, LANES))
            sv = jnp.broadcast_to(s1[:, v : v + 1], (count, LANES))
            cos_ref[:, v * LANES : (v + 1) * LANES] = cv * c2 - sv * s2
            sin_ref[:, v * LANES : (v + 1) * LANES] = sv * c2 + cv * s2

    def strip(v, carry):
        cols = pl.ds(pl.multiple_of(v * LANES, LANES), LANES)
        fc, fs = fine_cos[:, cols], fine_sin[:, cols]
        for u in range(coarse):
            cc = jnp.broadcast_to(coarse_cos[u : u + 1, cols], (FINE, LANES))
            cs = jnp.broadcast_to(coarse_sin[u : u + 1, cols], (FINE, LANES))
            table_ref[u * FINE : (u + 1) * FINE, cols] = (cc * fc - cs * fs).astype(jnp.bfloat16)
        return carry

    lax.fori_loop(0, strips, strip, 0)

    row = lax.broadcasted_iota(jnp.int32, (LANES, LANES), 0)
    col = lax.broadcasted_iota(jnp.int32, (LANES, LANES), 1)
    before = jnp.zeros((LANES, LANES), jnp.float32)
    per = BLOCK // LANES
    for e in range(1 - per, strips):
        if e < 0:
            tile = jnp.zeros((LANES, LANES), jnp.bfloat16)
        else:
            spread = jnp.broadcast_to(g_ref[e : e + 1, :], (LANES, LANES))
            rolled = pltpu.roll(spread, 0, 1, stride=1, stride_axis=0)
            tile = jnp.where(col >= row, rolled, before).astype(jnp.bfloat16)
            before = rolled
        for c in range(per):
            r = strips - per + c - e
            if 0 <= r < strips:
                toeplitz_ref[r * LANES : (r + 1) * LANES, c * LANES : (c + 1) * LANES] = tile

    quotes = maturity_ref.shape[1]
    last = jnp.broadcast_to(maturity_ref[...], (LANES, quotes))
    place = lax.broadcasted_iota(jnp.int32, (LANES, quotes), 0)
    for n in range(strips):
        mask_ref[n * LANES : (n + 1) * LANES, :] = jnp.where(place + n * LANES <= last, 1.0, 0.0).astype(jnp.bfloat16)


def driven(pieces, *refs):
    me_ref = refs[0]
    piece_refs = refs[1 : 1 + pieces]
    table_ref, toeplitz_ref, dw_ref, volterra_ref, weights = refs[1 + pieces :]
    steps = table_ref.shape[0]
    width = steps // pieces
    me = me_ref[0]
    for r in range(pieces):
        at = pl.multiple_of((me ^ r) * width, LANES)
        weights[:, pl.ds(at, width)] = piece_refs[r][...]
    blocks = steps // BLOCK
    for n in range(blocks):
        cols = slice(n * BLOCK, (n + 1) * BLOCK)
        dw_ref[:, cols] = jnp.dot(weights[...], table_ref[:, cols], preferred_element_type=jnp.float32).astype(jnp.bfloat16)
    for n in range(blocks):
        depth = (n + 1) * BLOCK
        volterra_ref[:, n * BLOCK : depth] = jnp.dot(
            dw_ref[:, :depth], toeplitz_ref[steps - depth :, :], preferred_element_type=jnp.float32
        )


def split(values):
    high = values.astype(jnp.bfloat16)
    return high, (values - high.astype(jnp.float32)).astype(jnp.bfloat16)


def priced(pieces, *refs):
    me_ref, scalar_ref = refs[:2]
    orth_refs = refs[2 : 2 + pieces]
    dw_ref, volterra_ref, mask_ref, strike_ref, sums_ref, own_ref, entering_ref, high, low, curve = refs[2 + pieces :]
    rows, steps = dw_ref.shape
    width = steps // pieces
    me = me_ref[0]
    half_eta, rho, orth_scale, half_step = (scalar_ref[n] for n in range(4))
    entering = jnp.zeros((rows, LANES), jnp.float32)
    for r in range(pieces):
        block = me ^ r
        extra = orth_refs[r][rows : rows + 16, :].astype(jnp.float32)
        curve[...] = extra[0:1, :] + extra[1:2, :] + extra[2:3, :]
        for n in range(width // BLOCK):
            cols = slice(n * BLOCK, (n + 1) * BLOCK)
            at = pl.ds(pl.multiple_of(block * width + n * BLOCK, BLOCK), BLOCK)
            root = jnp.exp(half_eta * volterra_ref[:, at] + curve[:, cols])
            noise = rho * dw_ref[:, at].astype(jnp.float32) + orth_scale * orth_refs[r][:rows, cols].astype(jnp.float32)
            increment = root * (noise - half_step * root)
            hi, lo = split(increment)
            high[:, at] = hi
            low[:, at] = lo
            if r == 0:
                own_ref[:, cols] = increment
            else:
                folded = functools.reduce(
                    lambda a, b: a + b, [increment[:, k * LANES : (k + 1) * LANES] for k in range(BLOCK // LANES)]
                )
                entering = entering + jnp.where(block < me, folded, 0.0)
    entering_ref[...] = entering
    picked = jnp.dot(high[...], mask_ref[...], preferred_element_type=jnp.float32) + jnp.dot(
        low[...], mask_ref[...], preferred_element_type=jnp.float32
    )
    payoff = jnp.maximum(jnp.exp(picked) - strike_ref[...], 0.0)
    sums_ref[...] = jnp.sum(payoff, axis=0, keepdims=True)


def summed(own_ref, entering_ref, out_ref):
    width = own_ref.shape[1]
    row = lax.broadcasted_iota(jnp.int32, (BLOCK, BLOCK), 0)
    col = lax.broadcasted_iota(jnp.int32, (BLOCK, BLOCK), 1)
    upper = jnp.where(row <= col, 1.0, 0.0).astype(jnp.bfloat16)
    carry = jnp.sum(entering_ref[...], axis=1, keepdims=True)
    for n in range(width // BLOCK):
        cols = slice(n * BLOCK, (n + 1) * BLOCK)
        hi, lo = split(own_ref[:, cols])
        total = carry + (
            jnp.dot(hi, upper, preferred_element_type=jnp.float32) + jnp.dot(lo, upper, preferred_element_type=jnp.float32)
        )
        out_ref[:, cols] = total
        carry = total[:, BLOCK - 1 :]


VMEM = pl.BlockSpec(memory_space=pltpu.VMEM)
SMEM = pl.BlockSpec(memory_space=pltpu.SMEM)


def kernel_of_lag(hurst_value, steps):
    lag = jnp.arange(steps, dtype=jnp.int32)
    expo = hurst_value - 0.5
    safe = jnp.maximum(lag, 1).astype(jnp.float32)
    inner = -jnp.expm1((expo + 1.0) * jnp.log1p(-1.0 / safe))
    log_b = ((expo + 1.0) * jnp.log(safe) + jnp.log(inner) - jnp.log(expo + 1.0)) / expo
    values = jnp.sqrt(2.0 * hurst_value) * jnp.exp(expo * (log_b + math.log(HORIZON / steps)))
    return jnp.where(lag >= 1, values, 0.0).reshape(steps // LANES, LANES)


def gather(value, axis):
    count = lax.axis_size(axis)
    held = [value] + [None] * (count - 1)
    dist = count // 2
    known = [0]
    while dist:
        pairs = [(n, n ^ dist) for n in range(count)]
        for r in list(known):
            held[r ^ dist] = lax.ppermute(held[r], axis, pairs)
        known += [r ^ dist for r in known]
        dist //= 2
    return held


def total_over(value, axis):
    count = lax.axis_size(axis)
    if count & (count - 1):
        return lax.psum(value, axis)
    dist = 1
    while dist < count:
        value = value + lax.ppermute(value, axis, [(n, n ^ dist) for n in range(count)])
        dist *= 2
    return value


def three_pieces(values):
    high = lax.reduce_precision(values, 8, 7)
    rest = values - high
    middle = lax.reduce_precision(rest, 8, 7)
    return [piece.astype(jnp.bfloat16) for piece in (high, middle, rest - middle)]


def on_device(normals, orth_normals, forward_var, hurst, eta, rho, strike_index, maturity_index):
    rows, width = normals.shape
    pieces = lax.axis_size("tm")
    steps = width * pieces
    step = HORIZON / steps
    quotes = strike_index.shape[0]
    me = lax.axis_index("tm").astype(jnp.int32)
    hurst_value, eta_value, rho_value = hurst[0], eta[0], rho[0]

    times = (me * width + jnp.arange(width, dtype=jnp.int32)).astype(jnp.float32) * step
    curve = 0.5 * jnp.log(forward_var) - 0.25 * eta_value * eta_value * times ** (2.0 * hurst_value)
    extra = jnp.stack(three_pieces(curve) + [jnp.zeros((width,), jnp.bfloat16)] * 13)
    orth = jnp.concatenate([orth_normals, extra], axis=0)
    weight_pieces = gather(normals, "tm")
    orth_pieces = gather(orth, "tm")

    table, toeplitz, mask = pl.pallas_call(
        functools.partial(prepare, steps),
        out_shape=(
            jax.ShapeDtypeStruct((steps, steps), jnp.bfloat16),
            jax.ShapeDtypeStruct((steps, BLOCK), jnp.bfloat16),
            jax.ShapeDtypeStruct((steps, quotes), jnp.bfloat16),
        ),
        in_specs=[VMEM] * 3,
        out_specs=(VMEM,) * 3,
        scratch_shapes=[pltpu.VMEM((FINE, steps), jnp.float32)] * 2 + [pltpu.VMEM((steps // FINE, steps), jnp.float32)] * 2,
        compiler_params=pltpu.CompilerParams(vmem_limit_bytes=24 << 20),
        cost_estimate=pl.CostEstimate(flops=4 * steps * steps, bytes_accessed=4 * steps * steps, transcendentals=0),
        name="prepare",
    )(jnp.asarray(base_angles(steps)), kernel_of_lag(hurst_value, steps), maturity_index.reshape(1, quotes))

    place = me.reshape(1)
    dw, volterra = pl.pallas_call(
        functools.partial(driven, pieces),
        out_shape=(jax.ShapeDtypeStruct((rows, steps), jnp.bfloat16), jax.ShapeDtypeStruct((rows, steps), jnp.float32)),
        in_specs=[SMEM] + [VMEM] * (pieces + 2),
        out_specs=(VMEM,) * 2,
        scratch_shapes=[pltpu.VMEM((rows, steps), jnp.bfloat16)],
        compiler_params=pltpu.CompilerParams(vmem_limit_bytes=24 << 20),
        cost_estimate=pl.CostEstimate(flops=3 * rows * steps * steps, bytes_accessed=2 * steps * steps, transcendentals=0),
        name="driven",
    )(place, *weight_pieces, table, toeplitz)

    scalars = jnp.stack([0.5 * eta_value, rho_value, jnp.sqrt(1.0 - rho_value * rho_value) * math.sqrt(step), jnp.float32(0.5 * step)])
    strikes = 0.5 + strike_index.astype(jnp.float32) / (STRIKES - 1)
    sums, own, entering = pl.pallas_call(
        functools.partial(priced, pieces),
        out_shape=(
            jax.ShapeDtypeStruct((1, quotes), jnp.float32),
            jax.ShapeDtypeStruct((rows, width), jnp.float32),
            jax.ShapeDtypeStruct((rows, LANES), jnp.float32),
        ),
        in_specs=[SMEM] * 2 + [VMEM] * (pieces + 4),
        out_specs=(VMEM,) * 3,
        scratch_shapes=[pltpu.VMEM((rows, steps), jnp.bfloat16)] * 2 + [pltpu.VMEM((1, width), jnp.float32)],
        compiler_params=pltpu.CompilerParams(vmem_limit_bytes=24 << 20),
        cost_estimate=pl.CostEstimate(flops=4 * rows * steps * quotes, bytes_accessed=8 * rows * steps, transcendentals=rows * steps),
        name="priced",
    )(place, scalars, *orth_pieces, dw, volterra, mask, strikes.reshape(1, quotes))

    log_price = pl.pallas_call(
        summed,
        out_shape=jax.ShapeDtypeStruct((rows, width), jnp.float32),
        in_specs=[VMEM] * 2,
        out_specs=VMEM,
        cost_estimate=pl.CostEstimate(flops=4 * rows * width * BLOCK, bytes_accessed=8 * rows * width, transcendentals=0),
        name="summed",
    )(own, entering)

    prices = total_over(sums, "path").reshape(quotes) / (rows * lax.axis_size("path"))
    return (log_price, prices)


def solution(mesh):
    in_specs = (
        P(("set", "path"), "tm"),
        P(("set", "path"), "tm"),
        P(("set", "tm")),
        P("set"),
        P("set"),
        P("set"),
        P("set"),
        P("set"),
    )
    out_specs = (P(("set", "path"), "tm"), P("set"))
    return jax.shard_map(on_device, mesh=mesh, in_specs=in_specs, out_specs=out_specs, check_vma=False)
```

```python
import functools
import math

import jax
import jax.numpy as jnp
import numpy as np
from jax import lax
from jax.experimental import pallas as pl
from jax.experimental.pallas import tpu as pltpu
from jax.sharding import PartitionSpec as P

STRIKES = 11
HORIZON = 2.0
LANES = 128
BLOCK = 256
EXTRA = 16
FINE = 64


def base_angles(steps):
    period = 4 * (2 * steps + 1)
    fine = 2 * np.arange(FINE) + 1
    coarse = 2 * FINE * np.arange(steps // FINE)
    lane = 2 * np.arange(LANES) + 1
    strip = 2 * LANES * np.arange(LANES)
    rows = []
    for left in (fine, coarse):
        for right in (strip, lane):
            turns = (left[:, None] * right[None, :]) % period
            angle = np.pi * turns / (2 * (2 * steps + 1))
            rows += [np.cos(angle), np.sin(angle)]
    return np.concatenate(rows, axis=0).astype(np.float32)


def fetch(sems, *pairs):
    copies = [pltpu.make_async_copy(source, target, sems.at[n]) for n, (source, target) in enumerate(pairs)]
    for copy in copies:
        copy.start()
    return copies


def packed(orth_hbm, forward_hbm, out_ref, forward, sems):
    rows, width = orth_hbm.shape
    big, small = fetch(sems, (orth_hbm, out_ref.at[:rows]), (forward_hbm, forward))
    small.wait()
    curve = 0.5 * jnp.log(forward[...])
    high = curve.astype(jnp.bfloat16).astype(jnp.float32)
    middle = (curve - high).astype(jnp.bfloat16).astype(jnp.float32)
    low = curve - high - middle
    row = lax.broadcasted_iota(jnp.int32, (EXTRA, width), 0)
    extra = jnp.where(row == 0, high, jnp.where(row == 1, middle, jnp.where(row == 2, low, 0.0)))
    out_ref[rows:, :] = extra.astype(jnp.bfloat16)
    big.wait()


def series(x, coefficients):
    total = jnp.full_like(x, coefficients[-1])
    for coefficient in coefficients[-2::-1]:
        total = total * x + coefficient
    return total


def lag_values(hurst_value, strips, steps):
    shape = (strips, LANES)
    lag = lax.broadcasted_iota(jnp.int32, shape, 0) * LANES + lax.broadcasted_iota(jnp.int32, shape, 1)
    hurst_all = jnp.broadcast_to(hurst_value, shape)
    expo = hurst_all - 0.5
    safe = jnp.maximum(lag, 1).astype(jnp.float32)
    odd = 1.0 / (2.0 * safe - 1.0)
    exponent = -2.0 * (expo + 1.0) * odd * series(odd * odd, [1.0 / (2 * n + 1) for n in range(9)])
    near = -exponent * series(exponent, [1.0 / math.factorial(n + 1) for n in range(11)])
    inner = jnp.where(lag >= 2, jnp.where(exponent > -0.7, near, 1.0 - jnp.exp(exponent)), 1.0)
    log_b = ((expo + 1.0) * jnp.log(safe) + jnp.log(inner) - jnp.log(expo + 1.0)) / expo
    values = jnp.sqrt(2.0 * hurst_all) * jnp.exp(expo * (log_b + math.log(HORIZON / steps)))
    return jnp.where(lag >= 1, values, 0.0)


def prepare(
    steps, scalar_ref, base_hbm, maturity_hbm, strike_hbm, own_hbm,
    table_ref, toeplitz_ref, mask_ref, decay_ref, strike_ref, own_ref,
    base_ref, maturity, strike, fine_cos, fine_sin, coarse_cos, coarse_sin, sems,
):
    coarse = steps // FINE
    strips = steps // LANES
    step = HORIZON / steps
    scale = math.sqrt(step) * 2.0 / math.sqrt(2 * steps + 1)
    copies = fetch(sems, (base_hbm, base_ref), (maturity_hbm, maturity), (strike_hbm, strike), (own_hbm, own_ref))
    hurst, eta = (scalar_ref[n : n + 1, :] for n in range(2))
    for n in range(strips):
        cols = slice(n * LANES, (n + 1) * LANES)
        times = (n * LANES + lax.broadcasted_iota(jnp.int32, (1, LANES), 1)).astype(jnp.float32) * step
        power = jnp.where(times > 0.0, jnp.exp(2.0 * hurst * jnp.log(times)), 0.0)
        decay_ref[:, cols] = -0.25 * eta * eta * power
    for copy in copies:
        copy.wait()
    strike_ref[...] = 0.5 + strike[...].astype(jnp.float32) / (STRIKES - 1)

    at = 0
    for count, cos_ref, sin_ref, factor in ((FINE, fine_cos, fine_sin, None), (coarse, coarse_cos, coarse_sin, scale)):
        c1, s1, c2, s2 = (base_ref[at + n * count : at + (n + 1) * count, :] for n in range(4))
        at += 4 * count
        if factor is not None:
            c2, s2 = c2 * factor, s2 * factor
        for v in range(strips):
            cv = jnp.broadcast_to(c1[:, v : v + 1], (count, LANES))
            sv = jnp.broadcast_to(s1[:, v : v + 1], (count, LANES))
            cos_ref[:, v * LANES : (v + 1) * LANES] = cv * c2 - sv * s2
            sin_ref[:, v * LANES : (v + 1) * LANES] = sv * c2 + cv * s2

    def strip(v, carry):
        cols = pl.ds(pl.multiple_of(v * LANES, LANES), LANES)
        fc, fs = fine_cos[:, cols], fine_sin[:, cols]
        for u in range(coarse):
            cc = jnp.broadcast_to(coarse_cos[u : u + 1, cols], (FINE, LANES))
            cs = jnp.broadcast_to(coarse_sin[u : u + 1, cols], (FINE, LANES))
            table_ref[u * FINE : (u + 1) * FINE, cols] = (cc * fc - cs * fs).astype(jnp.bfloat16)
        return carry

    lax.fori_loop(0, strips, strip, 0)

    lags = lag_values(hurst, strips, steps)
    row = lax.broadcasted_iota(jnp.int32, (LANES, LANES), 0)
    col = lax.broadcasted_iota(jnp.int32, (LANES, LANES), 1)
    before = jnp.zeros((LANES, LANES), jnp.float32)
    per = BLOCK // LANES
    for e in range(1 - per, strips):
        if e < 0:
            tile = jnp.zeros((LANES, LANES), jnp.bfloat16)
        else:
            spread = jnp.broadcast_to(lags[e : e + 1, :], (LANES, LANES))
            rolled = pltpu.roll(spread, 0, 1, stride=1, stride_axis=0)
            tile = jnp.where(col >= row, rolled, before).astype(jnp.bfloat16)
            before = rolled
        for c in range(per):
            r = strips - per + c - e
            if 0 <= r < strips:
                toeplitz_ref[r * LANES : (r + 1) * LANES, c * LANES : (c + 1) * LANES] = tile

    quotes = maturity.shape[1]
    last = jnp.broadcast_to(maturity[...], (LANES, quotes))
    place = lax.broadcasted_iota(jnp.int32, (LANES, quotes), 0)
    for n in range(strips):
        mask_ref[n * LANES : (n + 1) * LANES, :] = jnp.where(place + n * LANES <= last, 1.0, 0.0).astype(jnp.bfloat16)


def driven(pieces, axis, *refs):
    piece_refs = refs[:pieces]
    table_ref, toeplitz_ref, dw_ref, volterra_ref, weights = refs[pieces:]
    steps = table_ref.shape[0]
    width = steps // pieces
    me = lax.axis_index(axis)
    for r in range(pieces):
        at = pl.multiple_of((me ^ r) * width, LANES)
        weights[:, pl.ds(at, width)] = piece_refs[r][...]
    blocks = steps // BLOCK
    for n in range(blocks):
        cols = slice(n * BLOCK, (n + 1) * BLOCK)
        dw_ref[:, cols] = jnp.dot(weights[...], table_ref[:, cols], preferred_element_type=jnp.float32).astype(jnp.bfloat16)
    for n in range(blocks):
        depth = (n + 1) * BLOCK
        volterra_ref[:, n * BLOCK : depth] = jnp.dot(
            dw_ref[:, :depth], toeplitz_ref[steps - depth :, :], preferred_element_type=jnp.float32
        )


def split(values):
    high = values.astype(jnp.bfloat16)
    return high, (values - high.astype(jnp.float32)).astype(jnp.bfloat16)


def priced(pieces, axis, *refs):
    scalar_ref, decay_ref = refs[:2]
    orth_refs = refs[2 : 2 + pieces]
    dw_ref, volterra_ref, mask_ref, strike_ref, sums_ref, own_ref, entering_ref, high, low, curve = refs[2 + pieces :]
    rows, steps = dw_ref.shape
    width = steps // pieces
    me = lax.axis_index(axis)
    eta, rho = (jnp.broadcast_to(scalar_ref[n : n + 1, :1], (1, BLOCK)) for n in (1, 2))
    half_eta = 0.5 * eta
    orth_scale = jnp.sqrt(1.0 - rho * rho) * math.sqrt(HORIZON / steps)
    half_step = 0.5 * HORIZON / steps
    entering = jnp.zeros((rows, LANES), jnp.float32)
    for r in range(pieces):
        block = me ^ r
        extra = orth_refs[r][rows : rows + EXTRA, :].astype(jnp.float32)
        first = pl.multiple_of(block * width, BLOCK)
        curve[...] = extra[0:1, :] + extra[1:2, :] + extra[2:3, :] + decay_ref[:, pl.ds(first, width)]
        for n in range(width // BLOCK):
            cols = slice(n * BLOCK, (n + 1) * BLOCK)
            at = pl.ds(pl.multiple_of(block * width + n * BLOCK, BLOCK), BLOCK)
            root = jnp.exp(half_eta * volterra_ref[:, at] + curve[:, cols])
            noise = rho * dw_ref[:, at].astype(jnp.float32) + orth_scale * orth_refs[r][:rows, cols].astype(jnp.float32)
            increment = root * (noise - half_step * root)
            hi, lo = split(increment)
            high[:, at] = hi
            low[:, at] = lo
            if r == 0:
                own_ref[:, cols] = increment
            else:
                folded = functools.reduce(
                    lambda a, b: a + b, [increment[:, k * LANES : (k + 1) * LANES] for k in range(BLOCK // LANES)]
                )
                entering = entering + jnp.where(block < me, folded, 0.0)
    entering_ref[...] = entering
    picked = jnp.dot(high[...], mask_ref[...], preferred_element_type=jnp.float32) + jnp.dot(
        low[...], mask_ref[...], preferred_element_type=jnp.float32
    )
    payoff = jnp.maximum(jnp.exp(picked) - strike_ref[...], 0.0)
    sums_ref[...] = jnp.sum(payoff, axis=0, keepdims=True)


def summed(own_ref, entering_ref, out_ref):
    width = own_ref.shape[1]
    row = lax.broadcasted_iota(jnp.int32, (BLOCK, BLOCK), 0)
    col = lax.broadcasted_iota(jnp.int32, (BLOCK, BLOCK), 1)
    upper = jnp.where(row <= col, 1.0, 0.0).astype(jnp.bfloat16)
    carry = jnp.sum(entering_ref[...], axis=1, keepdims=True)
    for n in range(width // BLOCK):
        cols = slice(n * BLOCK, (n + 1) * BLOCK)
        hi, lo = split(own_ref[:, cols])
        total = carry + (
            jnp.dot(hi, upper, preferred_element_type=jnp.float32) + jnp.dot(lo, upper, preferred_element_type=jnp.float32)
        )
        out_ref[:, cols] = total
        carry = total[:, BLOCK - 1 :]


VMEM = pl.BlockSpec(memory_space=pltpu.VMEM)
HBM = pl.BlockSpec(memory_space=pltpu.HBM)


def gather(value, axis):
    count = lax.axis_size(axis)
    held = [value] + [None] * (count - 1)
    dist = count // 2
    known = [0]
    while dist:
        pairs = [(n, n ^ dist) for n in range(count)]
        for r in list(known):
            held[r ^ dist] = lax.ppermute(held[r], axis, pairs)
        known += [r ^ dist for r in known]
        dist //= 2
    return held


def total_over(value, axis):
    count = lax.axis_size(axis)
    if count & (count - 1):
        return lax.psum(value, axis)
    dist = 1
    while dist < count:
        value = value + lax.ppermute(value, axis, [(n, n ^ dist) for n in range(count)])
        dist *= 2
    return value


def stay(value):
    return pltpu.with_memory_space_constraint(value, pltpu.HBM)


def limit(mib):
    return pltpu.CompilerParams(vmem_limit_bytes=mib << 20)


def on_device(normals, orth_normals, forward_var, hurst, eta, rho, strike_index, maturity_index):
    rows, width = normals.shape
    pieces = lax.axis_size("tm")
    steps = width * pieces
    quotes = strike_index.shape[0]
    strips, coarse = steps // LANES, steps // FINE
    scalars = jnp.concatenate([jnp.broadcast_to(value, (1, LANES)) for value in (hurst, eta, rho)])
    forward_row, strike_row, maturity_row = (value.reshape(1, -1) for value in (forward_var, strike_index, maturity_index))

    weight_pieces = gather(normals, "tm")

    orth = pl.pallas_call(
        packed,
        out_shape=jax.ShapeDtypeStruct((rows + EXTRA, width), jnp.bfloat16),
        in_specs=[HBM] * 2,
        out_specs=VMEM,
        scratch_shapes=[pltpu.VMEM((1, width), jnp.float32), pltpu.SemaphoreType.DMA((2,))],
        compiler_params=limit(4),
        cost_estimate=pl.CostEstimate(flops=width, bytes_accessed=2 * rows * width, transcendentals=width),
        name="packed",
    )(stay(orth_normals), stay(forward_row))
    orth_pieces = gather(orth, "tm")

    base = base_angles(steps)
    table, toeplitz, mask, decay, strikes, own_weights = pl.pallas_call(
        functools.partial(prepare, steps),
        out_shape=(
            jax.ShapeDtypeStruct((steps, steps), jnp.bfloat16),
            jax.ShapeDtypeStruct((steps, BLOCK), jnp.bfloat16),
            jax.ShapeDtypeStruct((steps, quotes), jnp.bfloat16),
            jax.ShapeDtypeStruct((1, steps), jnp.float32),
            jax.ShapeDtypeStruct((1, quotes), jnp.float32),
            jax.ShapeDtypeStruct((rows, width), jnp.bfloat16),
        ),
        in_specs=[VMEM] + [HBM] * 4,
        out_specs=(VMEM,) * 6,
        scratch_shapes=[pltpu.VMEM(base.shape, jnp.float32)]
        + [pltpu.VMEM((1, quotes), jnp.int32)] * 2
        + [pltpu.VMEM((FINE, steps), jnp.float32)] * 2
        + [pltpu.VMEM((coarse, steps), jnp.float32)] * 2
        + [pltpu.SemaphoreType.DMA((4,))],
        compiler_params=limit(24),
        cost_estimate=pl.CostEstimate(flops=4 * steps * steps, bytes_accessed=4 * steps * steps, transcendentals=0),
        name="prepare",
    )(scalars, *map(stay, (jnp.asarray(base), maturity_row, strike_row, normals)))

    dw, volterra = pl.pallas_call(
        functools.partial(driven, pieces, "tm"),
        out_shape=(jax.ShapeDtypeStruct((rows, steps), jnp.bfloat16), jax.ShapeDtypeStruct((rows, steps), jnp.float32)),
        in_specs=[VMEM] * (pieces + 2),
        out_specs=(VMEM,) * 2,
        scratch_shapes=[pltpu.VMEM((rows, steps), jnp.bfloat16)],
        compiler_params=limit(24),
        cost_estimate=pl.CostEstimate(flops=3 * rows * steps * steps, bytes_accessed=2 * steps * steps, transcendentals=0),
        name="driven",
    )(own_weights, *weight_pieces[1:], table, toeplitz)

    sums, own, entering = pl.pallas_call(
        functools.partial(priced, pieces, "tm"),
        out_shape=(
            jax.ShapeDtypeStruct((1, quotes), jnp.float32),
            jax.ShapeDtypeStruct((rows, width), jnp.float32),
            jax.ShapeDtypeStruct((rows, LANES), jnp.float32),
        ),
        in_specs=[VMEM] * (pieces + 6),
        out_specs=(VMEM,) * 3,
        scratch_shapes=[pltpu.VMEM((rows, steps), jnp.bfloat16)] * 2 + [pltpu.VMEM((1, width), jnp.float32)],
        compiler_params=limit(24),
        cost_estimate=pl.CostEstimate(flops=4 * rows * steps * quotes, bytes_accessed=8 * rows * steps, transcendentals=rows * steps),
        name="priced",
    )(scalars, decay, *orth_pieces, dw, volterra, mask, strikes)

    log_price = pl.pallas_call(
        summed,
        out_shape=jax.ShapeDtypeStruct((rows, width), jnp.float32),
        in_specs=[VMEM] * 2,
        out_specs=VMEM,
        compiler_params=limit(4),
        cost_estimate=pl.CostEstimate(flops=4 * rows * width * BLOCK, bytes_accessed=8 * rows * width, transcendentals=0),
        name="summed",
    )(own, entering)

    prices = total_over(sums, "path").reshape(quotes) / (rows * lax.axis_size("path"))
    return (log_price, prices)


def solution(mesh):
    in_specs = (
        P(("set", "path"), "tm"),
        P(("set", "path"), "tm"),
        P(("set", "tm")),
        P("set"),
        P("set"),
        P("set"),
        P("set"),
        P("set"),
    )
    out_specs = (P(("set", "path"), "tm"), P("set"))
    return jax.shard_map(on_device, mesh=mesh, in_specs=in_specs, out_specs=out_specs, check_vma=False)
```

```python
import functools
import math

import jax
import jax.numpy as jnp
import numpy as np
from jax import lax
from jax.experimental import pallas as pl
from jax.experimental.pallas import tpu as pltpu
from jax.sharding import PartitionSpec as P

STRIKES = 11
HORIZON = 2.0
LANES = 128
BLOCK = 256
EXTRA = 16
FINE = 64


def seeds(steps):
    odd_col = 2 * np.arange(steps) + 1
    middle = steps // FINE // 2 - 1
    odd_row = 2 * np.arange(middle * FINE, (middle + 2) * FINE) + 1
    period = 4 * (2 * steps + 1)
    scale = math.sqrt(HORIZON / steps) * 2.0 / math.sqrt(2 * steps + 1)

    def cosine(turns):
        return np.cos(np.pi * (turns % period) / (2 * (2 * steps + 1)))

    strips = steps // LANES
    rows = (scale * cosine(odd_row[:, None] * odd_col[None, :])).reshape(2 * FINE, strips, LANES).transpose(1, 0, 2)
    factor = (2.0 * cosine(2 * FINE * odd_col)).reshape(strips, 1, LANES).repeat(8, axis=1)
    return np.concatenate([rows, factor], axis=1).astype(np.float32)


def fetch(sems, *pairs):
    copies = [pltpu.make_async_copy(source, target, sems.at[n]) for n, (source, target) in enumerate(pairs)]
    for copy in copies:
        copy.start()
    return copies


def tabled(seed_hbm, orth_hbm, forward_hbm, own_hbm, table_ref, out_ref, own_ref, seed, forward, sems):
    rows, width = orth_hbm.shape
    strips, steps, _ = table_ref.shape
    blocks = steps // FINE
    first, *others = fetch(
        sems, (seed_hbm, seed), (orth_hbm, out_ref.at[:rows]), (forward_hbm, forward), (own_hbm, own_ref)
    )
    first.wait()

    def strip(v, carry):
        factor = jnp.broadcast_to(seed[v, 2 * FINE : 2 * FINE + 1, :], (FINE, LANES))
        above, below = seed[v, :FINE, :], seed[v, FINE : 2 * FINE, :]
        low_pair, high_pair = (below, above), (above, below)
        middle = blocks // 2 - 1
        table_ref[v, middle * FINE : (middle + 1) * FINE, :] = above.astype(jnp.bfloat16)
        table_ref[v, (middle + 1) * FINE : (middle + 2) * FINE, :] = below.astype(jnp.bfloat16)
        for n in range(1, middle + 1):
            low_pair = (low_pair[1], factor * low_pair[1] - low_pair[0])
            high_pair = (high_pair[1], factor * high_pair[1] - high_pair[0])
            for at, value in ((middle - n, low_pair[1]), (middle + 1 + n, high_pair[1])):
                table_ref[v, at * FINE : (at + 1) * FINE, :] = value.astype(jnp.bfloat16)
        return carry

    lax.fori_loop(0, strips, strip, 0)
    for copy in others:
        copy.wait()
    curve = 0.5 * jnp.log(forward[...])
    high = curve.astype(jnp.bfloat16).astype(jnp.float32)
    middle = (curve - high).astype(jnp.bfloat16).astype(jnp.float32)
    low = curve - high - middle
    row = lax.broadcasted_iota(jnp.int32, (EXTRA, width), 0)
    extra = jnp.where(row == 0, high, jnp.where(row == 1, middle, jnp.where(row == 2, low, 0.0)))
    out_ref[rows:, :] = extra.astype(jnp.bfloat16)


def series(x, coefficients):
    total = jnp.full_like(x, coefficients[-1])
    for coefficient in coefficients[-2::-1]:
        total = total * x + coefficient
    return total


def lag_values(hurst_value, strips, steps):
    shape = (strips, LANES)
    lag = lax.broadcasted_iota(jnp.int32, shape, 0) * LANES + lax.broadcasted_iota(jnp.int32, shape, 1)
    hurst_all = jnp.broadcast_to(hurst_value, shape)
    expo = hurst_all - 0.5
    safe = jnp.maximum(lag, 1).astype(jnp.float32)
    odd = 1.0 / (2.0 * safe - 1.0)
    exponent = -2.0 * (expo + 1.0) * odd * series(odd * odd, [1.0 / (2 * n + 1) for n in range(9)])
    near = -exponent * series(exponent, [1.0 / math.factorial(n + 1) for n in range(11)])
    inner = jnp.where(lag >= 2, jnp.where(exponent > -0.7, near, 1.0 - jnp.exp(exponent)), 1.0)
    log_b = ((expo + 1.0) * jnp.log(safe) + jnp.log(inner) - jnp.log(expo + 1.0)) / expo
    values = jnp.sqrt(2.0 * hurst_all) * jnp.exp(expo * (log_b + math.log(HORIZON / steps)))
    return jnp.where(lag >= 1, values, 0.0)


def prepare(steps, hurst_ref, maturity_hbm, strike_hbm, toeplitz_ref, mask_ref, power_ref, strike_ref, maturity, strike, sems):
    strips = steps // LANES
    copies = fetch(sems, (maturity_hbm, maturity), (strike_hbm, strike))
    hurst = jnp.full((1, LANES), hurst_ref[0], jnp.float32)
    for n in range(strips):
        cols = slice(n * LANES, (n + 1) * LANES)
        times = (n * LANES + lax.broadcasted_iota(jnp.int32, (1, LANES), 1)).astype(jnp.float32) * (HORIZON / steps)
        power_ref[:, cols] = jnp.where(times > 0.0, jnp.exp(2.0 * hurst * jnp.log(times)), 0.0)

    lags = lag_values(hurst, strips, steps)
    row = lax.broadcasted_iota(jnp.int32, (LANES, LANES), 0)
    col = lax.broadcasted_iota(jnp.int32, (LANES, LANES), 1)
    before = jnp.zeros((LANES, LANES), jnp.float32)
    per = BLOCK // LANES
    for e in range(1 - per, strips):
        if e < 0:
            tile = jnp.zeros((LANES, LANES), jnp.bfloat16)
        else:
            spread = jnp.broadcast_to(lags[e : e + 1, :], (LANES, LANES))
            rolled = pltpu.roll(spread, 0, 1, stride=1, stride_axis=0)
            tile = jnp.where(col >= row, rolled, before).astype(jnp.bfloat16)
            before = rolled
        for c in range(per):
            r = strips - per + c - e
            if 0 <= r < strips:
                toeplitz_ref[r * LANES : (r + 1) * LANES, c * LANES : (c + 1) * LANES] = tile

    for copy in copies:
        copy.wait()
    strike_ref[...] = 0.5 + strike[...].astype(jnp.float32) / (STRIKES - 1)
    quotes = maturity.shape[1]
    last = jnp.broadcast_to(maturity[...], (LANES, quotes))
    place = lax.broadcasted_iota(jnp.int32, (LANES, quotes), 0)
    for n in range(strips):
        mask_ref[n * LANES : (n + 1) * LANES, :] = jnp.where(place + n * LANES <= last, 1.0, 0.0).astype(jnp.bfloat16)


def driven(pieces, axis, *refs):
    piece_refs = refs[:pieces]
    table_ref, toeplitz_ref, dw_ref, volterra_ref, weights = refs[pieces:]
    steps = table_ref.shape[1]
    width = steps // pieces
    me = lax.axis_index(axis)
    for r in range(pieces):
        at = pl.multiple_of((me ^ r) * width, LANES)
        weights[:, pl.ds(at, width)] = piece_refs[r][...]
    blocks = steps // BLOCK
    for n in range(blocks):
        per = BLOCK // LANES
        block = jnp.concatenate([table_ref[n * per + k] for k in range(per)], axis=1)
        dw = jnp.dot(weights[...], block, preferred_element_type=jnp.float32)
        dw_ref[:, n * BLOCK : (n + 1) * BLOCK] = dw.astype(jnp.bfloat16)
    for n in range(blocks):
        depth = (n + 1) * BLOCK
        volterra_ref[:, n * BLOCK : depth] = jnp.dot(
            dw_ref[:, :depth], toeplitz_ref[steps - depth :, :], preferred_element_type=jnp.float32
        )


def split(values):
    high = values.astype(jnp.bfloat16)
    return high, (values - high.astype(jnp.float32)).astype(jnp.bfloat16)


def priced(pieces, axis, *refs):
    eta_ref, rho_ref, power_ref = refs[:3]
    orth_refs = refs[3 : 3 + pieces]
    dw_ref, volterra_ref, mask_ref, strike_ref, sums_ref, own_ref, entering_ref, high, low, curve = refs[3 + pieces :]
    rows, steps = dw_ref.shape
    width = steps // pieces
    me = lax.axis_index(axis)
    rho = jnp.full((1, BLOCK), rho_ref[0], jnp.float32)
    half_eta = 0.5 * eta_ref[0]
    orth_scale = jnp.sqrt(1.0 - rho * rho) * math.sqrt(HORIZON / steps)
    half_step = 0.5 * HORIZON / steps
    entering = jnp.zeros((rows, LANES), jnp.float32)
    for r in range(pieces):
        block = me ^ r
        extra = orth_refs[r][rows : rows + EXTRA, :].astype(jnp.float32)
        first = pl.multiple_of(block * width, BLOCK)
        decay = half_eta * half_eta * power_ref[:, pl.ds(first, width)]
        curve[...] = extra[0:1, :] + extra[1:2, :] + extra[2:3, :] - decay
        for n in range(width // BLOCK):
            cols = slice(n * BLOCK, (n + 1) * BLOCK)
            at = pl.ds(pl.multiple_of(block * width + n * BLOCK, BLOCK), BLOCK)
            root = jnp.exp(half_eta * volterra_ref[:, at] + curve[:, cols])
            noise = rho * dw_ref[:, at].astype(jnp.float32) + orth_scale * orth_refs[r][:rows, cols].astype(jnp.float32)
            increment = root * (noise - half_step * root)
            hi, lo = split(increment)
            high[:, at] = hi
            low[:, at] = lo
            if r == 0:
                own_ref[:, cols] = increment
            else:
                folded = functools.reduce(
                    lambda a, b: a + b, [increment[:, k * LANES : (k + 1) * LANES] for k in range(BLOCK // LANES)]
                )
                entering = entering + jnp.where(block < me, folded, 0.0)
    entering_ref[...] = entering
    picked = jnp.dot(high[...], mask_ref[...], preferred_element_type=jnp.float32) + jnp.dot(
        low[...], mask_ref[...], preferred_element_type=jnp.float32
    )
    payoff = jnp.maximum(jnp.exp(picked) - strike_ref[...], 0.0)
    sums_ref[...] = jnp.sum(payoff, axis=0, keepdims=True)


def summed(own_ref, entering_ref, out_ref):
    width = own_ref.shape[1]
    row = lax.broadcasted_iota(jnp.int32, (BLOCK, BLOCK), 0)
    col = lax.broadcasted_iota(jnp.int32, (BLOCK, BLOCK), 1)
    upper = jnp.where(row <= col, 1.0, 0.0).astype(jnp.bfloat16)
    carry = jnp.sum(entering_ref[...], axis=1, keepdims=True)
    for n in range(width // BLOCK):
        cols = slice(n * BLOCK, (n + 1) * BLOCK)
        hi, lo = split(own_ref[:, cols])
        total = carry + (
            jnp.dot(hi, upper, preferred_element_type=jnp.float32) + jnp.dot(lo, upper, preferred_element_type=jnp.float32)
        )
        out_ref[:, cols] = total
        carry = total[:, BLOCK - 1 :]


VMEM = pl.BlockSpec(memory_space=pltpu.VMEM)
SMEM = pl.BlockSpec(memory_space=pltpu.SMEM)
HBM = pl.BlockSpec(memory_space=pltpu.HBM)


def gather(value, axis):
    count = lax.axis_size(axis)
    held = [value] + [None] * (count - 1)
    dist = count // 2
    known = [0]
    while dist:
        pairs = [(n, n ^ dist) for n in range(count)]
        for r in list(known):
            held[r ^ dist] = lax.ppermute(held[r], axis, pairs)
        known += [r ^ dist for r in known]
        dist //= 2
    return held


def total_over(value, axis):
    count = lax.axis_size(axis)
    if count & (count - 1):
        return lax.psum(value, axis)
    dist = 1
    while dist < count:
        value = value + lax.ppermute(value, axis, [(n, n ^ dist) for n in range(count)])
        dist *= 2
    return value


def stay(value):
    return pltpu.with_memory_space_constraint(value, pltpu.HBM)


def limit(mib):
    return pltpu.CompilerParams(vmem_limit_bytes=mib << 20)


def on_device(normals, orth_normals, forward_var, hurst, eta, rho, strike_index, maturity_index):
    rows, width = normals.shape
    pieces = lax.axis_size("tm")
    steps = width * pieces
    quotes = strike_index.shape[0]
    strips = steps // LANES
    forward_row, strike_row, maturity_row = (value.reshape(1, -1) for value in (forward_var, strike_index, maturity_index))

    weight_pieces = gather(normals, "tm")

    start = seeds(steps)
    table, orth, own_weights = pl.pallas_call(
        tabled,
        out_shape=(
            jax.ShapeDtypeStruct((strips, steps, LANES), jnp.bfloat16),
            jax.ShapeDtypeStruct((rows + EXTRA, width), jnp.bfloat16),
            jax.ShapeDtypeStruct((rows, width), jnp.bfloat16),
        ),
        in_specs=[HBM] * 4,
        out_specs=(VMEM,) * 3,
        scratch_shapes=[
            pltpu.VMEM(start.shape, jnp.float32),
            pltpu.VMEM((1, width), jnp.float32),
            pltpu.SemaphoreType.DMA((4,)),
        ],
        compiler_params=limit(16),
        cost_estimate=pl.CostEstimate(flops=4 * steps * steps, bytes_accessed=2 * steps * steps, transcendentals=width),
        name="tabled",
    )(*map(stay, (jnp.asarray(start), orth_normals, forward_row, normals)))
    orth_pieces = gather(orth, "tm")

    toeplitz, mask, power, strikes = pl.pallas_call(
        functools.partial(prepare, steps),
        out_shape=(
            jax.ShapeDtypeStruct((steps, BLOCK), jnp.bfloat16),
            jax.ShapeDtypeStruct((steps, quotes), jnp.bfloat16),
            jax.ShapeDtypeStruct((1, steps), jnp.float32),
            jax.ShapeDtypeStruct((1, quotes), jnp.float32),
        ),
        in_specs=[SMEM] + [HBM] * 2,
        out_specs=(VMEM,) * 4,
        scratch_shapes=[pltpu.VMEM((1, quotes), jnp.int32)] * 2 + [pltpu.SemaphoreType.DMA((2,))],
        compiler_params=limit(8),
        cost_estimate=pl.CostEstimate(flops=steps * BLOCK * 4, bytes_accessed=4 * steps * BLOCK, transcendentals=steps),
        name="prepare",
    )(hurst, stay(maturity_row), stay(strike_row))

    dw, volterra = pl.pallas_call(
        functools.partial(driven, pieces, "tm"),
        out_shape=(jax.ShapeDtypeStruct((rows, steps), jnp.bfloat16), jax.ShapeDtypeStruct((rows, steps), jnp.float32)),
        in_specs=[VMEM] * (pieces + 2),
        out_specs=(VMEM,) * 2,
        scratch_shapes=[pltpu.VMEM((rows, steps), jnp.bfloat16)],
        compiler_params=limit(24),
        cost_estimate=pl.CostEstimate(flops=3 * rows * steps * steps, bytes_accessed=2 * steps * steps, transcendentals=0),
        name="driven",
    )(own_weights, *weight_pieces[1:], table, toeplitz)

    sums, own, entering = pl.pallas_call(
        functools.partial(priced, pieces, "tm"),
        out_shape=(
            jax.ShapeDtypeStruct((1, quotes), jnp.float32),
            jax.ShapeDtypeStruct((rows, width), jnp.float32),
            jax.ShapeDtypeStruct((rows, LANES), jnp.float32),
        ),
        in_specs=[SMEM] * 2 + [VMEM] * (pieces + 5),
        out_specs=(VMEM,) * 3,
        scratch_shapes=[pltpu.VMEM((rows, steps), jnp.bfloat16)] * 2 + [pltpu.VMEM((1, width), jnp.float32)],
        compiler_params=limit(24),
        cost_estimate=pl.CostEstimate(flops=4 * rows * steps * quotes, bytes_accessed=8 * rows * steps, transcendentals=rows * steps),
        name="priced",
    )(eta, rho, power, *orth_pieces, dw, volterra, mask, strikes)

    log_price = pl.pallas_call(
        summed,
        out_shape=jax.ShapeDtypeStruct((rows, width), jnp.float32),
        in_specs=[VMEM] * 2,
        out_specs=VMEM,
        compiler_params=limit(4),
        cost_estimate=pl.CostEstimate(flops=4 * rows * width * BLOCK, bytes_accessed=8 * rows * width, transcendentals=0),
        name="summed",
    )(own, entering)

    prices = total_over(sums, "path").reshape(quotes) / (rows * lax.axis_size("path"))
    return (log_price, prices)


def solution(mesh):
    in_specs = (
        P(("set", "path"), "tm"),
        P(("set", "path"), "tm"),
        P(("set", "tm")),
        P("set"),
        P("set"),
        P("set"),
        P("set"),
        P("set"),
    )
    out_specs = (P(("set", "path"), "tm"), P("set"))
    return jax.shard_map(on_device, mesh=mesh, in_specs=in_specs, out_specs=out_specs, check_vma=False)
```

```python
import functools
import math

import jax
import jax.numpy as jnp
import numpy as np
from jax import lax
from jax.experimental import pallas as pl
from jax.experimental.pallas import tpu as pltpu
from jax.sharding import PartitionSpec as P

STRIKES = 11
HORIZON = 2.0
LANES = 128
BLOCK = 256
EXTRA = 16
FINE = 64


def seeds(steps):
    odd_col = 2 * np.arange(steps) + 1
    middle = steps // FINE // 2 - 1
    odd_row = 2 * np.arange(middle * FINE, (middle + 2) * FINE) + 1
    period = 4 * (2 * steps + 1)
    scale = math.sqrt(HORIZON / steps) * 2.0 / math.sqrt(2 * steps + 1)

    def cosine(turns):
        return np.cos(np.pi * (turns % period) / (2 * (2 * steps + 1)))

    strips = steps // LANES
    rows = (scale * cosine(odd_row[:, None] * odd_col[None, :])).reshape(2 * FINE, strips, LANES).transpose(1, 0, 2)
    factor = (2.0 * cosine(2 * FINE * odd_col)).reshape(strips, 1, LANES).repeat(8, axis=1)
    return np.concatenate([rows, factor], axis=1).astype(np.float32)


def fetch(sems, *pairs):
    copies = [pltpu.make_async_copy(source, target, sems.at[n]) for n, (source, target) in enumerate(pairs)]
    for copy in copies:
        copy.start()
    return copies


def fill(table_ref, seed, strips):
    blocks = table_ref.shape[1] // FINE
    middle = blocks // 2 - 1

    def strip(v, carry):
        factor = jnp.broadcast_to(seed[v, 2 * FINE : 2 * FINE + 1, :], (FINE, LANES))
        above, below = seed[v, :FINE, :], seed[v, FINE : 2 * FINE, :]
        low_pair, high_pair = (below, above), (above, below)
        table_ref[v, middle * FINE : (middle + 1) * FINE, :] = above.astype(jnp.bfloat16)
        table_ref[v, (middle + 1) * FINE : (middle + 2) * FINE, :] = below.astype(jnp.bfloat16)
        for n in range(1, middle + 1):
            low_pair = (low_pair[1], factor * low_pair[1] - low_pair[0])
            high_pair = (high_pair[1], factor * high_pair[1] - high_pair[0])
            for at, value in ((middle - n, low_pair[1]), (middle + 1 + n, high_pair[1])):
                table_ref[v, at * FINE : (at + 1) * FINE, :] = value.astype(jnp.bfloat16)
        return carry

    lax.fori_loop(*strips, strip, 0)


def series(x, coefficients):
    total = jnp.full_like(x, coefficients[-1])
    for coefficient in coefficients[-2::-1]:
        total = total * x + coefficient
    return total


def lag_values(hurst_all, strips, steps):
    shape = (strips, LANES)
    lag = lax.broadcasted_iota(jnp.int32, shape, 0) * LANES + lax.broadcasted_iota(jnp.int32, shape, 1)
    expo = hurst_all - 0.5
    safe = jnp.maximum(lag, 1).astype(jnp.float32)
    odd = 1.0 / (2.0 * safe - 1.0)
    exponent = -2.0 * (expo + 1.0) * odd * series(odd * odd, [1.0 / (2 * n + 1) for n in range(9)])
    near = -exponent * series(exponent, [1.0 / math.factorial(n + 1) for n in range(11)])
    inner = jnp.where(lag >= 2, jnp.where(exponent > -0.7, near, 1.0 - jnp.exp(exponent)), 1.0)
    log_b = ((expo + 1.0) * jnp.log(safe) + jnp.log(inner) - jnp.log(expo + 1.0)) / expo
    values = jnp.sqrt(2.0 * hurst_all) * jnp.exp(expo * (log_b + math.log(HORIZON / steps)))
    return jnp.where(lag >= 1, values, 0.0)


def spread_lags(lags, toeplitz_ref):
    strips = toeplitz_ref.shape[0] // LANES
    row = lax.broadcasted_iota(jnp.int32, (LANES, LANES), 0)
    col = lax.broadcasted_iota(jnp.int32, (LANES, LANES), 1)
    before = jnp.zeros((LANES, LANES), jnp.float32)
    per = BLOCK // LANES
    for e in range(1 - per, strips):
        if e < 0:
            tile = jnp.zeros((LANES, LANES), jnp.bfloat16)
        else:
            spread = jnp.broadcast_to(lags[e : e + 1, :], (LANES, LANES))
            rolled = pltpu.roll(spread, 0, 1, stride=1, stride_axis=0)
            tile = jnp.where(col >= row, rolled, before).astype(jnp.bfloat16)
            before = rolled
        for c in range(per):
            r = strips - per + c - e
            if 0 <= r < strips:
                toeplitz_ref[r * LANES : (r + 1) * LANES, c * LANES : (c + 1) * LANES] = tile


def packed(orth_hbm, forward_hbm, seed_hbm, maturity_hbm, strike_hbm, out_ref, seed_ref, maturity_ref, strike_ref, forward, sems):
    rows, width = orth_hbm.shape
    small, *others = fetch(
        sems, (forward_hbm, forward), (orth_hbm, out_ref.at[:rows]), (seed_hbm.at[: seed_ref.shape[0]], seed_ref),
        (maturity_hbm, maturity_ref), (strike_hbm, strike_ref),
    )
    small.wait()
    curve = 0.5 * jnp.log(forward[...])
    high = curve.astype(jnp.bfloat16).astype(jnp.float32)
    middle = (curve - high).astype(jnp.bfloat16).astype(jnp.float32)
    low = curve - high - middle
    row = lax.broadcasted_iota(jnp.int32, (EXTRA, width), 0)
    extra = jnp.where(row == 0, high, jnp.where(row == 1, middle, jnp.where(row == 2, low, 0.0)))
    out_ref[rows:, :] = extra.astype(jnp.bfloat16)
    for copy in others:
        copy.wait()


def prepare(
    hurst_ref, first_ref, maturity_ref, strike_ref, seed_hbm, own_hbm,
    table_ref, toeplitz_ref, power_ref, mask_ref, strikes_ref, own_ref, seed, sems,
):
    strips, steps, _ = table_ref.shape
    size = first_ref.shape[0]
    own, *copies = fetch(
        sems, (own_hbm, own_ref), *[(seed_hbm.at[n : n + size], seed.at[n : n + size]) for n in range(size, strips, size)]
    )
    fill(table_ref, first_ref, (0, size))
    hurst = jnp.full((strips, LANES), hurst_ref[0], jnp.float32)
    step = lax.broadcasted_iota(jnp.int32, hurst.shape, 0) * LANES + lax.broadcasted_iota(jnp.int32, hurst.shape, 1)
    times = step.astype(jnp.float32) * (HORIZON / steps)
    power = jnp.where(times > 0.0, jnp.exp(2.0 * hurst * jnp.log(times)), 0.0)
    for n in range(strips):
        power_ref[:, n * LANES : (n + 1) * LANES] = power[n : n + 1, :]
    spread_lags(lag_values(hurst, strips, steps), toeplitz_ref)
    strikes_ref[...] = 0.5 + strike_ref[...].astype(jnp.float32) / (STRIKES - 1)
    quotes = maturity_ref.shape[1]
    last = jnp.broadcast_to(maturity_ref[...], (LANES, quotes))
    place = lax.broadcasted_iota(jnp.int32, (LANES, quotes), 0)
    for n in range(strips):
        mask_ref[n * LANES : (n + 1) * LANES, :] = jnp.where(place + n * LANES <= last, 1.0, 0.0).astype(jnp.bfloat16)
    for n, copy in enumerate(copies):
        copy.wait()
        fill(table_ref, seed, ((n + 1) * size, (n + 2) * size))
    own.wait()


def products(pieces, table_ref, first, block):
    per = BLOCK // LANES
    total = None
    for r, piece_ref in pieces:
        width = piece_ref.shape[1]
        rows = pl.ds(pl.multiple_of((first ^ r) * width, LANES), width)
        columns = jnp.concatenate([table_ref[block * per + k, rows, :] for k in range(per)], axis=1)
        product = jnp.dot(piece_ref[...], columns, preferred_element_type=jnp.float32)
        total = product if total is None else total + product
    return total


def begun(axis, eta_ref, rho_ref, *refs):
    *piece_refs, table_ref, sum_ref, factor_ref = refs
    me = lax.axis_index(axis)
    steps = sum_ref.shape[1]
    rho = jnp.full(factor_ref.shape, rho_ref[0], jnp.float32)
    row = lax.broadcasted_iota(jnp.int32, factor_ref.shape, 0)
    orth_scale = jnp.sqrt(1.0 - rho * rho) * math.sqrt(HORIZON / steps)
    factor_ref[...] = jnp.where(row == 0, 0.5 * eta_ref[0], jnp.where(row == 1, rho, orth_scale))
    for n in range(steps // BLOCK):
        sum_ref[:, n * BLOCK : (n + 1) * BLOCK] = products(list(enumerate(piece_refs)), table_ref, me, n)


def driven(axis, *refs):
    sum_ref, *pieces = refs[:-4]
    table_ref, toeplitz_ref, dw_ref, volterra_ref = refs[-4:]
    steps = dw_ref.shape[1]
    me = lax.axis_index(axis)
    count = steps // pieces[0].shape[1] if pieces else 0
    held = [(count - len(pieces) + n, piece) for n, piece in enumerate(pieces)]
    blocks = steps // BLOCK
    for n in range(blocks):
        cols = slice(n * BLOCK, (n + 1) * BLOCK)
        dw = sum_ref[:, cols]
        if held:
            dw = dw + products(held, table_ref, me, n)
        dw_ref[:, cols] = dw.astype(jnp.bfloat16)
    for n in range(blocks):
        depth = (n + 1) * BLOCK
        volterra_ref[:, n * BLOCK : depth] = jnp.dot(
            dw_ref[:, :depth], toeplitz_ref[steps - depth :, :], preferred_element_type=jnp.float32
        )


def split(values):
    high = values.astype(jnp.bfloat16)
    return high, (values - high.astype(jnp.float32)).astype(jnp.bfloat16)


def priced(pieces, axis, *refs):
    factor_ref, power_ref = refs[:2]
    orth_refs = refs[2 : 2 + pieces]
    dw_ref, volterra_ref, mask_ref, strike_ref, sums_ref, own_ref, entering_ref, high, low, curve = refs[2 + pieces :]
    rows, steps = dw_ref.shape
    width = steps // pieces
    me = lax.axis_index(axis)
    half_eta, rho, orth_scale = (jnp.concatenate([factor_ref[n : n + 1, :]] * (BLOCK // LANES), axis=1) for n in range(3))
    half_step = 0.5 * HORIZON / steps
    entering = jnp.zeros((rows, LANES), jnp.float32)
    for r in range(pieces):
        block = me ^ r
        extra = orth_refs[r][rows : rows + EXTRA, :].astype(jnp.float32)
        first = pl.multiple_of(block * width, BLOCK)
        decay = half_eta[:, :1] * half_eta[:, :1] * power_ref[:, pl.ds(first, width)]
        curve[...] = extra[0:1, :] + extra[1:2, :] + extra[2:3, :] - decay
        for n in range(width // BLOCK):
            cols = slice(n * BLOCK, (n + 1) * BLOCK)
            at = pl.ds(pl.multiple_of(block * width + n * BLOCK, BLOCK), BLOCK)
            root = jnp.exp(half_eta * volterra_ref[:, at] + curve[:, cols])
            noise = rho * dw_ref[:, at].astype(jnp.float32) + orth_scale * orth_refs[r][:rows, cols].astype(jnp.float32)
            increment = root * (noise - half_step * root)
            hi, lo = split(increment)
            high[:, at] = hi
            low[:, at] = lo
            if r == 0:
                own_ref[:, cols] = increment
            else:
                folded = functools.reduce(
                    lambda a, b: a + b, [increment[:, k * LANES : (k + 1) * LANES] for k in range(BLOCK // LANES)]
                )
                entering = entering + jnp.where(block < me, folded, 0.0)
    entering_ref[...] = entering
    picked = jnp.dot(high[...], mask_ref[...], preferred_element_type=jnp.float32) + jnp.dot(
        low[...], mask_ref[...], preferred_element_type=jnp.float32
    )
    payoff = jnp.maximum(jnp.exp(picked) - strike_ref[...], 0.0)
    sums_ref[...] = jnp.sum(payoff, axis=0, keepdims=True)


def summed(own_ref, entering_ref, out_ref):
    width = own_ref.shape[1]
    row = lax.broadcasted_iota(jnp.int32, (BLOCK, BLOCK), 0)
    col = lax.broadcasted_iota(jnp.int32, (BLOCK, BLOCK), 1)
    upper = jnp.where(row <= col, 1.0, 0.0).astype(jnp.bfloat16)
    carry = jnp.sum(entering_ref[...], axis=1, keepdims=True)
    for n in range(width // BLOCK):
        cols = slice(n * BLOCK, (n + 1) * BLOCK)
        hi, lo = split(own_ref[:, cols])
        total = carry + (
            jnp.dot(hi, upper, preferred_element_type=jnp.float32) + jnp.dot(lo, upper, preferred_element_type=jnp.float32)
        )
        out_ref[:, cols] = total
        carry = total[:, BLOCK - 1 :]


VMEM = pl.BlockSpec(memory_space=pltpu.VMEM)
SMEM = pl.BlockSpec(memory_space=pltpu.SMEM)
HBM = pl.BlockSpec(memory_space=pltpu.HBM)


def swap(held, axis, dists):
    pairs = lambda dist: [(n, n ^ dist) for n in range(lax.axis_size(axis))]
    for dist in dists:
        held = held | {r ^ dist: lax.ppermute(piece, axis, pairs(dist)) for r, piece in held.items()}
    return held


def total_over(value, axis):
    count = lax.axis_size(axis)
    if count & (count - 1):
        return lax.psum(value, axis)
    dist = 1
    while dist < count:
        value = value + lax.ppermute(value, axis, [(n, n ^ dist) for n in range(count)])
        dist *= 2
    return value


def stay(value):
    return pltpu.with_memory_space_constraint(value, pltpu.HBM)


def limit(mib):
    return pltpu.CompilerParams(vmem_limit_bytes=mib << 20)


def on_device(normals, orth_normals, forward_var, hurst, eta, rho, strike_index, maturity_index):
    rows, width = normals.shape
    pieces = lax.axis_size("tm")
    steps = width * pieces
    quotes = strike_index.shape[0]
    strips = steps // LANES
    forward_row, strike_row, maturity_row = (value.reshape(1, -1) for value in (forward_var, strike_index, maturity_index))

    dists = [pieces >> n for n in range(1, pieces.bit_length())]
    held = swap({0: normals}, "tm", dists[:1])

    start = jnp.asarray(seeds(steps))
    size = math.gcd(strips, 4)
    held_seeds = (size,) + start.shape[1:]
    orth, first_seeds, maturity_held, strike_held = pl.pallas_call(
        packed,
        out_shape=(
            jax.ShapeDtypeStruct((rows + EXTRA, width), jnp.bfloat16),
            jax.ShapeDtypeStruct(held_seeds, jnp.float32),
            jax.ShapeDtypeStruct((1, quotes), jnp.int32),
            jax.ShapeDtypeStruct((1, quotes), jnp.int32),
        ),
        in_specs=[HBM] * 5,
        out_specs=(VMEM,) * 4,
        scratch_shapes=[pltpu.VMEM((1, width), jnp.float32), pltpu.SemaphoreType.DMA((5,))],
        compiler_params=limit(4),
        cost_estimate=pl.CostEstimate(flops=width, bytes_accessed=4 * rows * width, transcendentals=width),
        name="packed",
    )(*map(stay, (orth_normals, forward_row, start, maturity_row, strike_row)))
    orth_held = swap({0: orth}, "tm", dists[:1])

    table, toeplitz, power, mask, strikes, own_weights = pl.pallas_call(
        prepare,
        out_shape=(
            jax.ShapeDtypeStruct((strips, steps, LANES), jnp.bfloat16),
            jax.ShapeDtypeStruct((steps, BLOCK), jnp.bfloat16),
            jax.ShapeDtypeStruct((1, steps), jnp.float32),
            jax.ShapeDtypeStruct((steps, quotes), jnp.bfloat16),
            jax.ShapeDtypeStruct((1, quotes), jnp.float32),
            jax.ShapeDtypeStruct((rows, width), jnp.bfloat16),
        ),
        in_specs=[SMEM] + [VMEM] * 3 + [HBM] * 2,
        out_specs=(VMEM,) * 6,
        scratch_shapes=[pltpu.VMEM(start.shape, jnp.float32), pltpu.SemaphoreType.DMA((strips,))],
        compiler_params=limit(20),
        cost_estimate=pl.CostEstimate(flops=4 * steps * steps, bytes_accessed=2 * steps * steps, transcendentals=steps),
        name="prepare",
    )(hurst, first_seeds, maturity_held, strike_held, stay(start), stay(normals))

    far = {r: piece for r, piece in held.items() if r}
    far, strikes = lax.optimization_barrier((far, strikes))
    held = swap(held | far, "tm", dists[1:])
    weight_pieces = [own_weights] + [held[r] for r in range(1, pieces)]
    ready = max(pieces - 1, 1)

    sums, factors = pl.pallas_call(
        functools.partial(begun, "tm"),
        out_shape=(jax.ShapeDtypeStruct((rows, steps), jnp.float32), jax.ShapeDtypeStruct((8, LANES), jnp.float32)),
        in_specs=[SMEM] * 2 + [VMEM] * (ready + 1),
        out_specs=(VMEM,) * 2,
        compiler_params=limit(8),
        cost_estimate=pl.CostEstimate(flops=2 * rows * steps * steps, bytes_accessed=2 * steps * steps, transcendentals=0),
        name="begun",
    )(eta, rho, *weight_pieces[:ready], table)

    far = {r: piece for r, piece in orth_held.items() if r}
    far, sums = lax.optimization_barrier((far, sums))
    orth_held = swap(orth_held | far, "tm", dists[1:])
    orth_pieces = [orth_held[r] for r in range(pieces)]

    dw, volterra = pl.pallas_call(
        functools.partial(driven, "tm"),
        out_shape=(jax.ShapeDtypeStruct((rows, steps), jnp.bfloat16), jax.ShapeDtypeStruct((rows, steps), jnp.float32)),
        in_specs=[VMEM] * (pieces - ready + 3),
        out_specs=(VMEM,) * 2,
        compiler_params=limit(16),
        cost_estimate=pl.CostEstimate(flops=2 * rows * steps * steps, bytes_accessed=2 * steps * steps, transcendentals=0),
        name="driven",
    )(sums, *weight_pieces[ready:], table, toeplitz)

    payoffs, own, entering = pl.pallas_call(
        functools.partial(priced, pieces, "tm"),
        out_shape=(
            jax.ShapeDtypeStruct((1, quotes), jnp.float32),
            jax.ShapeDtypeStruct((rows, width), jnp.float32),
            jax.ShapeDtypeStruct((rows, LANES), jnp.float32),
        ),
        in_specs=[VMEM] * (pieces + 6),
        out_specs=(VMEM,) * 3,
        scratch_shapes=[pltpu.VMEM((rows, steps), jnp.bfloat16)] * 2 + [pltpu.VMEM((1, width), jnp.float32)],
        compiler_params=limit(24),
        cost_estimate=pl.CostEstimate(flops=4 * rows * steps * quotes, bytes_accessed=8 * rows * steps, transcendentals=rows * steps),
        name="priced",
    )(factors, power, *orth_pieces, dw, volterra, mask, strikes)

    log_price = pl.pallas_call(
        summed,
        out_shape=jax.ShapeDtypeStruct((rows, width), jnp.float32),
        in_specs=[VMEM] * 2,
        out_specs=VMEM,
        compiler_params=limit(4),
        cost_estimate=pl.CostEstimate(flops=4 * rows * width * BLOCK, bytes_accessed=8 * rows * width, transcendentals=0),
        name="summed",
    )(own, entering)

    prices = total_over(payoffs, "path").reshape(quotes) / (rows * lax.axis_size("path"))
    return (log_price, prices)


def solution(mesh):
    in_specs = (
        P(("set", "path"), "tm"),
        P(("set", "path"), "tm"),
        P(("set", "tm")),
        P("set"),
        P("set"),
        P("set"),
        P("set"),
        P("set"),
    )
    out_specs = (P(("set", "path"), "tm"), P("set"))
    return jax.shard_map(on_device, mesh=mesh, in_specs=in_specs, out_specs=out_specs, check_vma=False)
```

```python
import functools
import math

import jax
import jax.numpy as jnp
import numpy as np
from jax import lax
from jax.experimental import pallas as pl
from jax.experimental.pallas import tpu as pltpu
from jax.sharding import PartitionSpec as P

STRIKES = 11
HORIZON = 2.0
LANES = 128
BLOCK = 256
EXTRA = 16
FINE = 64
COMPUTED = 2
EARLY = 6


def seeds(steps):
    odd_col = 2 * np.arange(steps) + 1
    middle = steps // FINE // 2 - 1
    odd_row = 2 * np.arange(middle * FINE, (middle + 2) * FINE) + 1
    period = 4 * (2 * steps + 1)
    scale = math.sqrt(HORIZON / steps) * 2.0 / math.sqrt(2 * steps + 1)

    def cosine(turns):
        return np.cos(np.pi * (turns % period) / (2 * (2 * steps + 1)))

    strips = steps // LANES
    rows = (scale * cosine(odd_row[:, None] * odd_col[None, :])).reshape(2 * FINE, strips, LANES).transpose(1, 0, 2)
    factor = (2.0 * cosine(2 * FINE * odd_col)).reshape(strips, 1, LANES).repeat(8, axis=1)
    return np.concatenate([rows, factor], axis=1).astype(np.float32)


def fetch(sems, *pairs):
    copies = [pltpu.make_async_copy(source, target, sems.at[n]) for n, (source, target) in enumerate(pairs)]
    for copy in copies:
        copy.start()
    return copies


def grow(table_ref, v, factor, above, below):
    middle = table_ref.shape[1] // FINE // 2 - 1
    low_pair, high_pair = (below, above), (above, below)
    table_ref[v, middle * FINE : (middle + 1) * FINE, :] = above.astype(jnp.bfloat16)
    table_ref[v, (middle + 1) * FINE : (middle + 2) * FINE, :] = below.astype(jnp.bfloat16)
    for n in range(1, middle + 1):
        low_pair = (low_pair[1], factor * low_pair[1] - low_pair[0])
        high_pair = (high_pair[1], factor * high_pair[1] - high_pair[0])
        for at, value in ((middle - n, low_pair[1]), (middle + 1 + n, high_pair[1])):
            table_ref[v, at * FINE : (at + 1) * FINE, :] = value.astype(jnp.bfloat16)


def fill(table_ref, first, seed, count):
    def strip(v, carry):
        factor = jnp.broadcast_to(seed[v, 2 * FINE : 2 * FINE + 1, :], (FINE, LANES))
        grow(table_ref, first + v, factor, seed[v, :FINE, :], seed[v, FINE : 2 * FINE, :])
        return carry

    lax.fori_loop(0, count, strip, 0)


def cosine(turns, period):
    rest = turns - period * jnp.floor(turns * (1.0 / period))
    angle = (jnp.abs(rest - period // 2) - period // 4) * (2.0 * math.pi / period)
    return angle * series(angle * angle, [(-1.0) ** n / math.factorial(2 * n + 1) for n in range(7)])


def fill_computed(table_ref, first, count):
    steps = table_ref.shape[1]
    period = 4 * (2 * steps + 1)
    scale = math.sqrt(HORIZON / steps) * 2.0 / math.sqrt(2 * steps + 1)
    middle = steps // FINE // 2 - 1
    assert (2 * (middle + 2) * FINE) * (2 * steps) < 2**24

    def odds(shape, axis, first):
        return (2 * (first + lax.broadcasted_iota(jnp.int32, shape, axis)) + 1).astype(jnp.float32)

    def strip(v, carry):
        cols = odds((FINE, LANES), 1, (first + v) * LANES)
        factor = jnp.broadcast_to(2.0 * cosine(2.0 * FINE * cols[:8, :], period)[:1, :], (FINE, LANES))
        above, below = (
            scale * cosine(odds((FINE, LANES), 0, (middle + n) * FINE) * cols, period) for n in range(2)
        )
        grow(table_ref, v, factor, above, below)
        return carry

    lax.fori_loop(0, count, strip, 0)


def series(x, coefficients):
    total = jnp.full_like(x, coefficients[-1])
    for coefficient in coefficients[-2::-1]:
        total = total * x + coefficient
    return total


def lag_values(hurst_all, strips, steps):
    shape = (strips, LANES)
    lag = lax.broadcasted_iota(jnp.int32, shape, 0) * LANES + lax.broadcasted_iota(jnp.int32, shape, 1)
    expo = hurst_all - 0.5
    safe = jnp.maximum(lag, 1).astype(jnp.float32)
    odd = 1.0 / (2.0 * safe - 1.0)
    exponent = -2.0 * (expo + 1.0) * odd * series(odd * odd, [1.0 / (2 * n + 1) for n in range(9)])
    near = -exponent * series(exponent, [1.0 / math.factorial(n + 1) for n in range(11)])
    inner = jnp.where(lag >= 2, jnp.where(exponent > -0.7, near, 1.0 - jnp.exp(exponent)), 1.0)
    log_b = ((expo + 1.0) * jnp.log(safe) + jnp.log(inner) - jnp.log(expo + 1.0)) / expo
    values = jnp.sqrt(2.0 * hurst_all) * jnp.exp(expo * (log_b + math.log(HORIZON / steps)))
    return jnp.where(lag >= 1, values, 0.0)


def spread_lags(lags, toeplitz_ref):
    strips = toeplitz_ref.shape[0] // LANES
    row = lax.broadcasted_iota(jnp.int32, (LANES, LANES), 0)
    col = lax.broadcasted_iota(jnp.int32, (LANES, LANES), 1)
    before = jnp.zeros((LANES, LANES), jnp.float32)
    per = BLOCK // LANES
    for e in range(1 - per, strips):
        if e < 0:
            tile = jnp.zeros((LANES, LANES), jnp.bfloat16)
        else:
            spread = jnp.broadcast_to(lags[e : e + 1, :], (LANES, LANES))
            rolled = pltpu.roll(spread, 0, 1, stride=1, stride_axis=0)
            tile = jnp.where(col >= row, rolled, before).astype(jnp.bfloat16)
            before = rolled
        for c in range(per):
            r = strips - per + c - e
            if 0 <= r < strips:
                toeplitz_ref[r * LANES : (r + 1) * LANES, c * LANES : (c + 1) * LANES] = tile


def packed(orth_hbm, forward_hbm, out_ref, table_ref, forward, sems):
    rows, width = orth_hbm.shape
    small, *others = fetch(sems, (forward_hbm, forward), (orth_hbm, out_ref.at[:rows]))
    fill_computed(table_ref, 0, table_ref.shape[0])
    small.wait()
    curve = 0.5 * jnp.log(forward[...])
    high = curve.astype(jnp.bfloat16).astype(jnp.float32)
    middle = (curve - high).astype(jnp.bfloat16).astype(jnp.float32)
    low = curve - high - middle
    row = lax.broadcasted_iota(jnp.int32, (EXTRA, width), 0)
    extra = jnp.where(row == 0, high, jnp.where(row == 1, middle, jnp.where(row == 2, low, 0.0)))
    out_ref[rows:, :] = extra.astype(jnp.bfloat16)
    for copy in others:
        copy.wait()


def prepare(
    hurst_ref, seed_hbm, own_hbm, maturity_hbm, strike_hbm,
    table_ref, toeplitz_ref, power_ref, mask_ref, strikes_ref, own_ref, maturity, strike, seed, sems,
):
    late, steps, _ = table_ref.shape
    strips = steps // LANES
    computed = min(COMPUTED, late)
    parts = [(n, min(4, late - n)) for n in range(computed, late, 4)]
    own, to_maturity, to_strike, *copies = fetch(
        sems, (own_hbm, own_ref), (maturity_hbm, maturity), (strike_hbm, strike),
        *[(seed_hbm.at[pl.ds(strips - late + n, count)], seed.at[pl.ds(n, count)]) for n, count in parts],
    )
    hurst = jnp.full((strips, LANES), hurst_ref[0], jnp.float32)
    step = lax.broadcasted_iota(jnp.int32, hurst.shape, 0) * LANES + lax.broadcasted_iota(jnp.int32, hurst.shape, 1)
    times = step.astype(jnp.float32) * (HORIZON / steps)
    power = jnp.where(times > 0.0, jnp.exp(2.0 * hurst * jnp.log(times)), 0.0)
    for n in range(strips):
        power_ref[:, n * LANES : (n + 1) * LANES] = power[n : n + 1, :]
    spread_lags(lag_values(hurst, strips, steps), toeplitz_ref)
    fill_computed(table_ref, strips - late, computed)
    to_maturity.wait()
    to_strike.wait()
    strikes_ref[...] = 0.5 + strike[...].astype(jnp.float32) / (STRIKES - 1)
    quotes = maturity.shape[1]
    last = jnp.broadcast_to(maturity[...], (LANES, quotes))
    place = lax.broadcasted_iota(jnp.int32, (LANES, quotes), 0)
    for n in range(strips):
        mask_ref[n * LANES : (n + 1) * LANES, :] = jnp.where(place + n * LANES <= last, 1.0, 0.0).astype(jnp.bfloat16)
    for (n, count), copy in zip(parts, copies):
        copy.wait()
        fill(table_ref, n, seed.at[pl.ds(n, count)], count)
    own.wait()


def products(pieces, table_refs, first, block):
    per = BLOCK // LANES
    strips = [(ref, n) for ref in table_refs for n in range(ref.shape[0])][block * per : (block + 1) * per]
    total = None
    for r, piece_ref in pieces:
        width = piece_ref.shape[1]
        rows = pl.ds(pl.multiple_of((first ^ r) * width, LANES), width)
        columns = jnp.concatenate([ref[n, rows, :] for ref, n in strips], axis=1)
        product = jnp.dot(piece_ref[...], columns, preferred_element_type=jnp.float32)
        total = product if total is None else total + product
    return total


def begun(axis, eta_ref, rho_ref, *refs):
    *piece_refs, early_ref, late_ref, sum_ref, factor_ref = refs
    me = lax.axis_index(axis)
    steps = sum_ref.shape[1]
    rho = jnp.full(factor_ref.shape, rho_ref[0], jnp.float32)
    row = lax.broadcasted_iota(jnp.int32, factor_ref.shape, 0)
    orth_scale = jnp.sqrt(1.0 - rho * rho) * math.sqrt(HORIZON / steps)
    factor_ref[...] = jnp.where(row == 0, 0.5 * eta_ref[0], jnp.where(row == 1, rho, orth_scale))
    for n in range(steps // BLOCK):
        sum_ref[:, n * BLOCK : (n + 1) * BLOCK] = products(list(enumerate(piece_refs)), (early_ref, late_ref), me, n)


def driven(axis, *refs):
    sum_ref, *pieces = refs[:-5]
    early_ref, late_ref, toeplitz_ref, dw_ref, volterra_ref = refs[-5:]
    steps = dw_ref.shape[1]
    me = lax.axis_index(axis)
    count = steps // pieces[0].shape[1] if pieces else 0
    held = [(count - len(pieces) + n, piece) for n, piece in enumerate(pieces)]
    blocks = steps // BLOCK
    for n in range(blocks):
        cols = slice(n * BLOCK, (n + 1) * BLOCK)
        dw = sum_ref[:, cols]
        if held:
            dw = dw + products(held, (early_ref, late_ref), me, n)
        dw_ref[:, cols] = dw.astype(jnp.bfloat16)
    for n in range(blocks):
        depth = (n + 1) * BLOCK
        volterra_ref[:, n * BLOCK : depth] = jnp.dot(
            dw_ref[:, :depth], toeplitz_ref[steps - depth :, :], preferred_element_type=jnp.float32
        )


def split(values):
    high = values.astype(jnp.bfloat16)
    return high, (values - high.astype(jnp.float32)).astype(jnp.bfloat16)


def priced(pieces, axis, *refs):
    factor_ref, power_ref = refs[:2]
    orth_refs = refs[2 : 2 + pieces]
    dw_ref, volterra_ref, mask_ref, strike_ref, sums_ref, own_ref, entering_ref, high, low, curve = refs[2 + pieces :]
    rows, steps = dw_ref.shape
    width = steps // pieces
    me = lax.axis_index(axis)
    half_eta, rho, orth_scale = (jnp.concatenate([factor_ref[n : n + 1, :]] * (BLOCK // LANES), axis=1) for n in range(3))
    half_step = 0.5 * HORIZON / steps
    entering = jnp.zeros((rows, LANES), jnp.float32)
    for r in range(pieces):
        block = me ^ r
        extra = orth_refs[r][rows : rows + EXTRA, :].astype(jnp.float32)
        first = pl.multiple_of(block * width, BLOCK)
        decay = half_eta[:, :1] * half_eta[:, :1] * power_ref[:, pl.ds(first, width)]
        curve[...] = extra[0:1, :] + extra[1:2, :] + extra[2:3, :] - decay
        for n in range(width // BLOCK):
            cols = slice(n * BLOCK, (n + 1) * BLOCK)
            at = pl.ds(pl.multiple_of(block * width + n * BLOCK, BLOCK), BLOCK)
            root = jnp.exp(half_eta * volterra_ref[:, at] + curve[:, cols])
            noise = rho * dw_ref[:, at].astype(jnp.float32) + orth_scale * orth_refs[r][:rows, cols].astype(jnp.float32)
            increment = root * (noise - half_step * root)
            hi, lo = split(increment)
            high[:, at] = hi
            low[:, at] = lo
            if r == 0:
                own_ref[:, cols] = increment
            else:
                folded = functools.reduce(
                    lambda a, b: a + b, [increment[:, k * LANES : (k + 1) * LANES] for k in range(BLOCK // LANES)]
                )
                entering = entering + jnp.where(block < me, folded, 0.0)
    entering_ref[...] = entering
    picked = jnp.dot(high[...], mask_ref[...], preferred_element_type=jnp.float32) + jnp.dot(
        low[...], mask_ref[...], preferred_element_type=jnp.float32
    )
    payoff = jnp.maximum(jnp.exp(picked) - strike_ref[...], 0.0)
    sums_ref[...] = jnp.sum(payoff, axis=0, keepdims=True)


def summed(own_ref, entering_ref, out_ref):
    width = own_ref.shape[1]
    row = lax.broadcasted_iota(jnp.int32, (BLOCK, BLOCK), 0)
    col = lax.broadcasted_iota(jnp.int32, (BLOCK, BLOCK), 1)
    upper = jnp.where(row <= col, 1.0, 0.0).astype(jnp.bfloat16)
    carry = jnp.sum(entering_ref[...], axis=1, keepdims=True)
    for n in range(width // BLOCK):
        cols = slice(n * BLOCK, (n + 1) * BLOCK)
        hi, lo = split(own_ref[:, cols])
        total = carry + (
            jnp.dot(hi, upper, preferred_element_type=jnp.float32) + jnp.dot(lo, upper, preferred_element_type=jnp.float32)
        )
        out_ref[:, cols] = total
        carry = total[:, BLOCK - 1 :]


VMEM = pl.BlockSpec(memory_space=pltpu.VMEM)
SMEM = pl.BlockSpec(memory_space=pltpu.SMEM)
HBM = pl.BlockSpec(memory_space=pltpu.HBM)


def swap(held, axis, dists):
    pairs = lambda dist: [(n, n ^ dist) for n in range(lax.axis_size(axis))]
    for dist in dists:
        held = held | {r ^ dist: lax.ppermute(piece, axis, pairs(dist)) for r, piece in held.items()}
    return held


def total_over(value, axis):
    count = lax.axis_size(axis)
    if count & (count - 1):
        return lax.psum(value, axis)
    dist = 1
    while dist < count:
        value = value + lax.ppermute(value, axis, [(n, n ^ dist) for n in range(count)])
        dist *= 2
    return value


def stay(value):
    return pltpu.with_memory_space_constraint(value, pltpu.HBM)


def limit(mib):
    return pltpu.CompilerParams(vmem_limit_bytes=mib << 20)


def on_device(normals, orth_normals, forward_var, hurst, eta, rho, strike_index, maturity_index):
    rows, width = normals.shape
    pieces = lax.axis_size("tm")
    steps = width * pieces
    quotes = strike_index.shape[0]
    strips = steps // LANES
    forward_row, strike_row, maturity_row = (value.reshape(1, -1) for value in (forward_var, strike_index, maturity_index))

    dists = [pieces >> n for n in range(1, pieces.bit_length())]
    held = swap({0: normals}, "tm", dists[:1])

    start = jnp.asarray(seeds(steps))
    early = strips * EARLY // 16
    orth, early_table = pl.pallas_call(
        packed,
        out_shape=(
            jax.ShapeDtypeStruct((rows + EXTRA, width), jnp.bfloat16),
            jax.ShapeDtypeStruct((early, steps, LANES), jnp.bfloat16),
        ),
        in_specs=[HBM] * 2,
        out_specs=(VMEM,) * 2,
        scratch_shapes=[pltpu.VMEM((1, width), jnp.float32), pltpu.SemaphoreType.DMA((2,))],
        compiler_params=limit(8),
        cost_estimate=pl.CostEstimate(flops=width, bytes_accessed=4 * rows * width, transcendentals=width),
        name="packed",
    )(stay(orth_normals), stay(forward_row))
    orth_held = swap({0: orth}, "tm", dists[:1])

    late_table, toeplitz, power, mask, strikes, own_weights = pl.pallas_call(
        prepare,
        out_shape=(
            jax.ShapeDtypeStruct((strips - early, steps, LANES), jnp.bfloat16),
            jax.ShapeDtypeStruct((steps, BLOCK), jnp.bfloat16),
            jax.ShapeDtypeStruct((1, steps), jnp.float32),
            jax.ShapeDtypeStruct((steps, quotes), jnp.bfloat16),
            jax.ShapeDtypeStruct((1, quotes), jnp.float32),
            jax.ShapeDtypeStruct((rows, width), jnp.bfloat16),
        ),
        in_specs=[SMEM] + [HBM] * 4,
        out_specs=(VMEM,) * 6,
        scratch_shapes=[pltpu.VMEM((1, quotes), jnp.int32)] * 2
        + [pltpu.VMEM(start.shape, jnp.float32), pltpu.SemaphoreType.DMA((strips + 3,))],
        compiler_params=limit(20),
        cost_estimate=pl.CostEstimate(flops=4 * steps * steps, bytes_accessed=2 * steps * steps, transcendentals=steps),
        name="prepare",
    )(hurst, *map(stay, (start, normals, maturity_row, strike_row)))

    far = {r: piece for r, piece in held.items() if r}
    far, strikes = lax.optimization_barrier((far, strikes))
    held = swap(held | far, "tm", dists[1:])
    weight_pieces = [own_weights] + [held[r] for r in range(1, pieces)]
    ready = max(pieces - 1, 1)

    sums, factors = pl.pallas_call(
        functools.partial(begun, "tm"),
        out_shape=(jax.ShapeDtypeStruct((rows, steps), jnp.float32), jax.ShapeDtypeStruct((8, LANES), jnp.float32)),
        in_specs=[SMEM] * 2 + [VMEM] * (ready + 2),
        out_specs=(VMEM,) * 2,
        compiler_params=limit(8),
        cost_estimate=pl.CostEstimate(flops=2 * rows * steps * steps, bytes_accessed=2 * steps * steps, transcendentals=0),
        name="begun",
    )(eta, rho, *weight_pieces[:ready], early_table, late_table)

    far = {r: piece for r, piece in orth_held.items() if r}
    far, sums = lax.optimization_barrier((far, sums))
    orth_held = swap(orth_held | far, "tm", dists[1:])
    orth_pieces = [orth_held[r] for r in range(pieces)]

    dw, volterra = pl.pallas_call(
        functools.partial(driven, "tm"),
        out_shape=(jax.ShapeDtypeStruct((rows, steps), jnp.bfloat16), jax.ShapeDtypeStruct((rows, steps), jnp.float32)),
        in_specs=[VMEM] * (pieces - ready + 4),
        out_specs=(VMEM,) * 2,
        compiler_params=limit(16),
        cost_estimate=pl.CostEstimate(flops=2 * rows * steps * steps, bytes_accessed=2 * steps * steps, transcendentals=0),
        name="driven",
    )(sums, *weight_pieces[ready:], early_table, late_table, toeplitz)

    payoffs, own, entering = pl.pallas_call(
        functools.partial(priced, pieces, "tm"),
        out_shape=(
            jax.ShapeDtypeStruct((1, quotes), jnp.float32),
            jax.ShapeDtypeStruct((rows, width), jnp.float32),
            jax.ShapeDtypeStruct((rows, LANES), jnp.float32),
        ),
        in_specs=[VMEM] * (pieces + 6),
        out_specs=(VMEM,) * 3,
        scratch_shapes=[pltpu.VMEM((rows, steps), jnp.bfloat16)] * 2 + [pltpu.VMEM((1, width), jnp.float32)],
        compiler_params=limit(24),
        cost_estimate=pl.CostEstimate(flops=4 * rows * steps * quotes, bytes_accessed=8 * rows * steps, transcendentals=rows * steps),
        name="priced",
    )(factors, power, *orth_pieces, dw, volterra, mask, strikes)

    log_price = pl.pallas_call(
        summed,
        out_shape=jax.ShapeDtypeStruct((rows, width), jnp.float32),
        in_specs=[VMEM] * 2,
        out_specs=VMEM,
        compiler_params=limit(4),
        cost_estimate=pl.CostEstimate(flops=4 * rows * width * BLOCK, bytes_accessed=8 * rows * width, transcendentals=0),
        name="summed",
    )(own, entering)

    prices = total_over(payoffs, "path").reshape(quotes) / (rows * lax.axis_size("path"))
    return (log_price, prices)


def solution(mesh):
    in_specs = (
        P(("set", "path"), "tm"),
        P(("set", "path"), "tm"),
        P(("set", "tm")),
        P("set"),
        P("set"),
        P("set"),
        P("set"),
        P("set"),
    )
    out_specs = (P(("set", "path"), "tm"), P("set"))
    return jax.shard_map(on_device, mesh=mesh, in_specs=in_specs, out_specs=out_specs, check_vma=False)
```

```python
import functools
import math

import jax
import jax.numpy as jnp
from jax import lax
from jax.experimental import pallas as pl
from jax.experimental.pallas import tpu as pltpu
from jax.sharding import PartitionSpec as P

STRIKES = 11
HORIZON = 2.0
LANES = 128
BLOCK = 256
EXTRA = 8
FINE = 64
MIDDLE = 6
EARLY = 6


def fetch(sems, *pairs):
    copies = [pltpu.make_async_copy(source, target, sems.at[n]) for n, (source, target) in enumerate(pairs)]
    for copy in copies:
        copy.start()
    return copies


def grow(table_ref, v, factor, above, below):
    middle = table_ref.shape[1] // FINE // 2 - 1
    low_pair, high_pair = (below, above), (above, below)
    table_ref[v, middle * FINE : (middle + 1) * FINE, :] = above.astype(jnp.bfloat16)
    table_ref[v, (middle + 1) * FINE : (middle + 2) * FINE, :] = below.astype(jnp.bfloat16)
    for n in range(1, middle + 1):
        low_pair = (low_pair[1], factor * low_pair[1] - low_pair[0])
        high_pair = (high_pair[1], factor * high_pair[1] - high_pair[0])
        for at, value in ((middle - n, low_pair[1]), (middle + 1 + n, high_pair[1])):
            table_ref[v, at * FINE : (at + 1) * FINE, :] = value.astype(jnp.bfloat16)


def cosine(turns, period):
    rest = turns - period * jnp.floor(turns * (1.0 / period))
    angle = (jnp.abs(rest - period // 2) - period // 4) * (2.0 * math.pi / period)
    return angle * series(angle * angle, [(-1.0) ** n / math.factorial(2 * n + 1) for n in range(7)])


def fill_computed(table_ref, first, count):
    steps = table_ref.shape[1]
    period = 4 * (2 * steps + 1)
    scale = math.sqrt(HORIZON / steps) * 2.0 / math.sqrt(2 * steps + 1)
    middle = steps // FINE // 2 - 1
    assert (2 * (middle + 2) * FINE) * (2 * steps) < 2**24

    def odds(shape, axis, first):
        return (2 * (first + lax.broadcasted_iota(jnp.int32, shape, axis)) + 1).astype(jnp.float32)

    def strip(v, carry):
        cols = odds((FINE, LANES), 1, (first + v) * LANES)
        factor = jnp.broadcast_to(2.0 * cosine(2.0 * FINE * cols[:8, :], period)[:1, :], (FINE, LANES))
        above, below = (
            scale * cosine(odds((FINE, LANES), 0, (middle + n) * FINE) * cols, period) for n in range(2)
        )
        grow(table_ref, v, factor, above, below)
        return carry

    lax.fori_loop(0, count, strip, 0)


def series(x, coefficients):
    total = jnp.full_like(x, coefficients[-1])
    for coefficient in coefficients[-2::-1]:
        total = total * x + coefficient
    return total


def lag_values(hurst_all, strips, steps):
    shape = (strips, LANES)
    lag = lax.broadcasted_iota(jnp.int32, shape, 0) * LANES + lax.broadcasted_iota(jnp.int32, shape, 1)
    expo = hurst_all - 0.5
    safe = jnp.maximum(lag, 1).astype(jnp.float32)
    odd = 1.0 / (2.0 * safe - 1.0)
    exponent = -2.0 * (expo + 1.0) * odd * series(odd * odd, [1.0 / (2 * n + 1) for n in range(9)])
    near = -exponent * series(exponent, [1.0 / math.factorial(n + 1) for n in range(11)])
    inner = jnp.where(lag >= 2, jnp.where(exponent > -0.7, near, 1.0 - jnp.exp(exponent)), 1.0)
    log_b = ((expo + 1.0) * jnp.log(safe) + jnp.log(inner) - jnp.log(expo + 1.0)) / expo
    values = jnp.sqrt(2.0 * hurst_all) * jnp.exp(expo * (log_b + math.log(HORIZON / steps)))
    return jnp.where(lag >= 1, values, 0.0)


def spread_lags(lags, toeplitz_ref):
    strips = toeplitz_ref.shape[0] // LANES
    row = lax.broadcasted_iota(jnp.int32, (LANES, LANES), 0)
    col = lax.broadcasted_iota(jnp.int32, (LANES, LANES), 1)
    before = jnp.zeros((LANES, LANES), jnp.float32)
    per = BLOCK // LANES
    for e in range(1 - per, strips):
        if e < 0:
            tile = jnp.zeros((LANES, LANES), jnp.bfloat16)
        else:
            spread = jnp.broadcast_to(lags[e : e + 1, :], (LANES, LANES))
            rolled = pltpu.roll(spread, 0, 1, stride=1, stride_axis=0)
            tile = jnp.where(col >= row, rolled, before).astype(jnp.bfloat16)
            before = rolled
        for c in range(per):
            r = strips - per + c - e
            if 0 <= r < strips:
                toeplitz_ref[r * LANES : (r + 1) * LANES, c * LANES : (c + 1) * LANES] = tile


def packed(orth_hbm, forward_hbm, out_ref, table_ref, forward, sems):
    rows, width = orth_hbm.shape
    small, *others = fetch(sems, (forward_hbm, forward), (orth_hbm, out_ref.at[:rows]))
    fill_computed(table_ref, 0, table_ref.shape[0])
    small.wait()
    curve = 0.5 * jnp.log(forward[...])
    high = curve.astype(jnp.bfloat16).astype(jnp.float32)
    middle = (curve - high).astype(jnp.bfloat16).astype(jnp.float32)
    low = curve - high - middle
    row = lax.broadcasted_iota(jnp.int32, (EXTRA, width), 0)
    extra = jnp.where(row == 0, high, jnp.where(row == 1, middle, jnp.where(row == 2, low, 0.0)))
    out_ref[rows:, :] = extra.astype(jnp.bfloat16)
    for copy in others:
        copy.wait()


def prepare(
    hurst_ref, eta_ref, rho_ref, own_hbm, maturity_hbm, strike_hbm,
    table_ref, toeplitz_ref, power_ref, factor_ref, own_ref, maturity_ref, strike_ref, sems,
):
    strips = power_ref.shape[1] // LANES
    steps = table_ref.shape[1]
    copies = fetch(sems, (own_hbm, own_ref), (maturity_hbm, maturity_ref), (strike_hbm, strike_ref))
    hurst = jnp.full((strips, LANES), hurst_ref[0], jnp.float32)
    step = lax.broadcasted_iota(jnp.int32, hurst.shape, 0) * LANES + lax.broadcasted_iota(jnp.int32, hurst.shape, 1)
    times = step.astype(jnp.float32) * (HORIZON / steps)
    power = jnp.where(times > 0.0, jnp.exp(2.0 * hurst * jnp.log(times)), 0.0)
    for n in range(strips):
        power_ref[:, n * LANES : (n + 1) * LANES] = power[n : n + 1, :]
    rho = jnp.full(factor_ref.shape, rho_ref[0], jnp.float32)
    row = lax.broadcasted_iota(jnp.int32, factor_ref.shape, 0)
    orth_scale = jnp.sqrt(1.0 - rho * rho) * math.sqrt(HORIZON / steps)
    factor_ref[...] = jnp.where(row == 0, 0.5 * eta_ref[0], jnp.where(row == 1, rho, orth_scale))
    spread_lags(lag_values(hurst, strips, steps), toeplitz_ref)
    fill_computed(table_ref, strips * EARLY // 16, table_ref.shape[0])
    for copy in copies:
        copy.wait()


def complete(maturity_ref, strike_ref, table_ref, mask_ref, strikes_ref):
    strips = mask_ref.shape[0] // LANES
    late = table_ref.shape[0]
    strikes_ref[...] = 0.5 + strike_ref[...].astype(jnp.float32) / (STRIKES - 1)
    quotes = maturity_ref.shape[1]
    last = jnp.broadcast_to(maturity_ref[...], (LANES, quotes))
    place = lax.broadcasted_iota(jnp.int32, (LANES, quotes), 0)
    for n in range(strips):
        mask_ref[n * LANES : (n + 1) * LANES, :] = jnp.where(place + n * LANES <= last, 1.0, 0.0).astype(jnp.bfloat16)
    fill_computed(table_ref, strips - late, late)


def products(pieces, table_refs, first, block):
    per = BLOCK // LANES
    strips = [(ref, n) for ref in table_refs for n in range(ref.shape[0])][block * per : (block + 1) * per]
    total = None
    for r, piece_ref in pieces:
        width = piece_ref.shape[1]
        rows = pl.ds(pl.multiple_of((first ^ r) * width, LANES), width)
        columns = jnp.concatenate([ref[n, rows, :] for ref, n in strips], axis=1)
        product = jnp.dot(piece_ref[...], columns, preferred_element_type=jnp.float32)
        total = product if total is None else total + product
    return total


def driven(axis, pieces, *refs):
    piece_refs = refs[:pieces]
    *table_refs, dw_ref = refs[pieces:]
    me = lax.axis_index(axis)
    steps = dw_ref.shape[1]
    for n in range(steps // BLOCK):
        dw = products(list(enumerate(piece_refs)), table_refs, me, n)
        dw_ref[:, n * BLOCK : (n + 1) * BLOCK] = dw.astype(jnp.bfloat16)


def split(values):
    high = values.astype(jnp.bfloat16)
    return high, (values - high.astype(jnp.float32)).astype(jnp.bfloat16)


def increments(factor_ref, decay_power, orth_ref, volterra, dw, cols):
    rows = volterra.shape[0]
    half_eta, rho, orth_scale = (jnp.concatenate([factor_ref[n : n + 1, :]] * (BLOCK // LANES), axis=1) for n in range(3))
    extra = orth_ref[rows : rows + EXTRA, cols].astype(jnp.float32)
    curve = extra[0:1, :] + extra[1:2, :] + extra[2:3, :] - half_eta * half_eta * decay_power
    root = jnp.exp(half_eta * volterra + curve)
    noise = rho * dw.astype(jnp.float32) + orth_scale * orth_ref[:rows, cols].astype(jnp.float32)
    return root, noise


def fold(increment, entering, enters):
    folded = functools.reduce(lambda a, b: a + b, [increment[:, k * LANES : (k + 1) * LANES] for k in range(BLOCK // LANES)])
    return entering + jnp.where(enters, folded, 0.0)


def moved(pieces, ready, axis, *refs):
    factor_ref, power_ref, dw_ref, toeplitz_ref, mask_ref = refs[:5]
    orth_refs = refs[5 : 5 + ready]
    own_ref, entering_ref, picked_ref, *rest_refs, volterra, high, low = refs[5 + ready :]
    rows, steps = dw_ref.shape
    width = steps // pieces
    half_step = 0.5 * HORIZON / steps
    me = lax.axis_index(axis)
    for n in range(steps // BLOCK):
        depth = (n + 1) * BLOCK
        volterra[:, n * BLOCK : depth] = jnp.dot(
            dw_ref[:, :depth], toeplitz_ref[steps - depth :, :], preferred_element_type=jnp.float32
        )
    entering = jnp.zeros((rows, LANES), jnp.float32)
    picked = jnp.zeros(picked_ref.shape, jnp.float32)
    for r in range(ready):
        block = me ^ r
        for n in range(width // BLOCK):
            cols = slice(n * BLOCK, (n + 1) * BLOCK)
            at = pl.ds(pl.multiple_of(block * width + n * BLOCK, BLOCK), BLOCK)
            root, noise = increments(factor_ref, power_ref[:, at], orth_refs[r], volterra[:, at], dw_ref[:, at], cols)
            increment = root * (noise - half_step * root)
            high[:, cols], low[:, cols] = split(increment)
            if r == 0:
                own_ref[:, cols] = increment
            else:
                entering = fold(increment, entering, block < me)
        until = mask_ref[pl.ds(pl.multiple_of(block * width, BLOCK), width), :]
        picked = picked + (
            jnp.dot(high[...], until, preferred_element_type=jnp.float32)
            + jnp.dot(low[...], until, preferred_element_type=jnp.float32)
        )
    for r, rest_ref in enumerate(rest_refs, ready):
        rest_ref[...] = volterra[:, pl.ds(pl.multiple_of((me ^ r) * width, BLOCK), width)]
    entering_ref[...] = entering
    picked_ref[...] = picked


def priced(pieces, ready, axis, *refs):
    rest = pieces - ready
    factor_ref, power_ref, dw_ref, mask_ref, strike_ref, before_ref, begun_ref = refs[:7]
    volterra_refs, orth_refs = refs[7 : 7 + rest], refs[7 + rest : 7 + 2 * rest]
    sums_ref, entering_ref, high, low = refs[7 + 2 * rest :]
    rows, steps = dw_ref.shape
    width = steps // pieces
    half_step = 0.5 * HORIZON / steps
    me = lax.axis_index(axis)
    entering = before_ref[...]
    picked = begun_ref[...]
    for r in range(ready, pieces):
        block = me ^ r
        for n in range(width // BLOCK):
            cols = slice(n * BLOCK, (n + 1) * BLOCK)
            at = pl.ds(pl.multiple_of(block * width + n * BLOCK, BLOCK), BLOCK)
            root, noise = increments(
                factor_ref, power_ref[:, at], orth_refs[r - ready], volterra_refs[r - ready][:, cols], dw_ref[:, at], cols
            )
            increment = root * (noise - half_step * root)
            high[:, cols], low[:, cols] = split(increment)
            entering = fold(increment, entering, block < me)
        until = mask_ref[pl.ds(pl.multiple_of(block * width, BLOCK), width), :]
        picked = picked + (
            jnp.dot(high[...], until, preferred_element_type=jnp.float32)
            + jnp.dot(low[...], until, preferred_element_type=jnp.float32)
        )
    entering_ref[...] = entering
    payoff = jnp.maximum(jnp.exp(picked) - strike_ref[...], 0.0)
    sums_ref[...] = jnp.sum(payoff, axis=0, keepdims=True)


def summed(own_ref, entering_ref, out_ref):
    width = own_ref.shape[1]
    row = lax.broadcasted_iota(jnp.int32, (BLOCK, BLOCK), 0)
    col = lax.broadcasted_iota(jnp.int32, (BLOCK, BLOCK), 1)
    upper = jnp.where(row <= col, 1.0, 0.0).astype(jnp.bfloat16)
    carry = jnp.sum(entering_ref[...], axis=1, keepdims=True)
    for n in range(width // BLOCK):
        cols = slice(n * BLOCK, (n + 1) * BLOCK)
        hi, lo = split(own_ref[:, cols])
        total = carry + (
            jnp.dot(hi, upper, preferred_element_type=jnp.float32) + jnp.dot(lo, upper, preferred_element_type=jnp.float32)
        )
        out_ref[:, cols] = total
        carry = total[:, BLOCK - 1 :]


VMEM = pl.BlockSpec(memory_space=pltpu.VMEM)
SMEM = pl.BlockSpec(memory_space=pltpu.SMEM)
HBM = pl.BlockSpec(memory_space=pltpu.HBM)


def swap(held, axis, dists):
    pairs = lambda dist: [(n, n ^ dist) for n in range(lax.axis_size(axis))]
    for dist in dists:
        held = held | {r ^ dist: lax.ppermute(piece, axis, pairs(dist)) for r, piece in held.items()}
    return held


def total_over(value, axis):
    count = lax.axis_size(axis)
    if count & (count - 1):
        return lax.psum(value, axis)
    dist = 1
    while dist < count:
        value = value + lax.ppermute(value, axis, [(n, n ^ dist) for n in range(count)])
        dist *= 2
    return value


def stay(value):
    return pltpu.with_memory_space_constraint(value, pltpu.HBM)


def limit(mib):
    return pltpu.CompilerParams(vmem_limit_bytes=mib << 20)


def on_device(normals, orth_normals, forward_var, hurst, eta, rho, strike_index, maturity_index):
    rows, width = normals.shape
    pieces = lax.axis_size("tm")
    steps = width * pieces
    quotes = strike_index.shape[0]
    strips = steps // LANES
    forward_row, strike_row, maturity_row = (value.reshape(1, -1) for value in (forward_var, strike_index, maturity_index))

    dists = [pieces >> n for n in range(1, pieces.bit_length())]
    held = swap({0: normals}, "tm", dists[:1])

    early = strips * EARLY // 16
    orth, early_table = pl.pallas_call(
        packed,
        out_shape=(
            jax.ShapeDtypeStruct((rows + EXTRA, width), jnp.bfloat16),
            jax.ShapeDtypeStruct((early, steps, LANES), jnp.bfloat16),
        ),
        in_specs=[HBM] * 2,
        out_specs=(VMEM,) * 2,
        scratch_shapes=[pltpu.VMEM((1, width), jnp.float32), pltpu.SemaphoreType.DMA((2,))],
        compiler_params=limit(8),
        cost_estimate=pl.CostEstimate(flops=width, bytes_accessed=4 * rows * width, transcendentals=width),
        name="packed",
    )(stay(orth_normals), stay(forward_row))
    early_table, strike_row = lax.optimization_barrier((early_table, strike_row))
    orth_held = swap({0: orth}, "tm", dists[:1])

    middle = min(MIDDLE * strips // 16, strips - early)
    late = strips - early - middle
    middle_table, toeplitz, power, factors, own_weights, maturity_held, strike_held = pl.pallas_call(
        prepare,
        out_shape=(
            jax.ShapeDtypeStruct((middle, steps, LANES), jnp.bfloat16),
            jax.ShapeDtypeStruct((steps, BLOCK), jnp.bfloat16),
            jax.ShapeDtypeStruct((1, steps), jnp.float32),
            jax.ShapeDtypeStruct((8, LANES), jnp.float32),
            jax.ShapeDtypeStruct((rows, width), jnp.bfloat16),
            jax.ShapeDtypeStruct((1, quotes), jnp.int32),
            jax.ShapeDtypeStruct((1, quotes), jnp.int32),
        ),
        in_specs=[SMEM] * 3 + [HBM] * 3,
        out_specs=(VMEM,) * 7,
        scratch_shapes=[pltpu.SemaphoreType.DMA((3,))],
        compiler_params=limit(8),
        cost_estimate=pl.CostEstimate(flops=steps * steps, bytes_accessed=steps * steps, transcendentals=steps),
        name="prepare",
    )(hurst, eta, rho, *map(stay, (normals, maturity_row, strike_row)))

    far = {r: piece for r, piece in held.items() if r}
    far, maturity_held = lax.optimization_barrier((far, maturity_held))
    held = swap(held | far, "tm", dists[1:])
    weight_pieces = [own_weights] + [held[r] for r in range(1, pieces)]

    late_table, mask, strikes = pl.pallas_call(
        complete,
        out_shape=(
            jax.ShapeDtypeStruct((late, steps, LANES), jnp.bfloat16),
            jax.ShapeDtypeStruct((steps, quotes), jnp.bfloat16),
            jax.ShapeDtypeStruct((1, quotes), jnp.float32),
        ),
        in_specs=[VMEM] * 2,
        out_specs=(VMEM,) * 3,
        compiler_params=limit(8),
        cost_estimate=pl.CostEstimate(flops=steps, bytes_accessed=steps, transcendentals=0),
        name="complete",
    )(maturity_held, strike_held)

    dw = pl.pallas_call(
        functools.partial(driven, "tm", pieces),
        out_shape=jax.ShapeDtypeStruct((rows, steps), jnp.bfloat16),
        in_specs=[VMEM] * (pieces + 3),
        out_specs=VMEM,
        compiler_params=limit(8),
        cost_estimate=pl.CostEstimate(flops=steps, bytes_accessed=steps, transcendentals=0),
        name="driven",
    )(*weight_pieces, early_table, middle_table, late_table)

    far = {r: piece for r, piece in orth_held.items() if r}
    far, dw = lax.optimization_barrier((far, dw))
    orth_held = swap(orth_held | far, "tm", dists[1:])
    orth_pieces = [orth_held[r] for r in range(pieces)]
    ready = max(pieces - 1, 1)
    rest = pieces - ready

    own, entering, picked, *volterra = pl.pallas_call(
        functools.partial(moved, pieces, ready, "tm"),
        out_shape=(
            jax.ShapeDtypeStruct((rows, width), jnp.float32),
            jax.ShapeDtypeStruct((rows, LANES), jnp.float32),
            jax.ShapeDtypeStruct((rows, quotes), jnp.float32),
        )
        + (jax.ShapeDtypeStruct((rows, width), jnp.float32),) * rest,
        in_specs=[VMEM] * (5 + ready),
        out_specs=(VMEM,) * (3 + rest),
        scratch_shapes=[pltpu.VMEM((rows, steps), jnp.float32)] + [pltpu.VMEM((rows, width), jnp.bfloat16)] * 2,
        compiler_params=limit(16),
        cost_estimate=pl.CostEstimate(flops=4 * rows * steps * quotes, bytes_accessed=8 * rows * steps, transcendentals=rows * steps),
        name="moved",
    )(factors, power, dw, toeplitz, mask, *orth_pieces[:ready])

    payoffs, entering = pl.pallas_call(
        functools.partial(priced, pieces, ready, "tm"),
        out_shape=(jax.ShapeDtypeStruct((1, quotes), jnp.float32), jax.ShapeDtypeStruct((rows, LANES), jnp.float32)),
        in_specs=[VMEM] * (7 + 2 * rest),
        out_specs=(VMEM,) * 2,
        scratch_shapes=[pltpu.VMEM((rows, width), jnp.bfloat16)] * 2,
        compiler_params=limit(8),
        cost_estimate=pl.CostEstimate(flops=rows * steps * quotes, bytes_accessed=2 * rows * steps, transcendentals=rows * width),
        name="priced",
    )(factors, power, dw, mask, strikes, entering, picked, *volterra, *orth_pieces[ready:])

    log_price = pl.pallas_call(
        summed,
        out_shape=jax.ShapeDtypeStruct((rows, width), jnp.float32),
        in_specs=[VMEM] * 2,
        out_specs=VMEM,
        compiler_params=limit(4),
        cost_estimate=pl.CostEstimate(flops=4 * rows * width * BLOCK, bytes_accessed=8 * rows * width, transcendentals=0),
        name="summed",
    )(own, entering)

    prices = total_over(payoffs, "path").reshape(quotes) / (rows * lax.axis_size("path"))
    return (log_price, prices)


def solution(mesh):
    in_specs = (
        P(("set", "path"), "tm"),
        P(("set", "path"), "tm"),
        P(("set", "tm")),
        P("set"),
        P("set"),
        P("set"),
        P("set"),
        P("set"),
    )
    out_specs = (P(("set", "path"), "tm"), P("set"))
    return jax.shard_map(on_device, mesh=mesh, in_specs=in_specs, out_specs=out_specs, check_vma=False)
```

```python
import functools
import math

import jax
import jax.numpy as jnp
from jax import lax
from jax.experimental import pallas as pl
from jax.experimental.pallas import tpu as pltpu
from jax.sharding import PartitionSpec as P

STRIKES = 11
HORIZON = 2.0
LANES = 128
BLOCK = 256
EXTRA = 8
FINE = 64
MIDDLE = 5
EARLY = 6


def fetch(sems, *pairs):
    copies = [pltpu.make_async_copy(source, target, sems.at[n]) for n, (source, target) in enumerate(pairs)]
    for copy in copies:
        copy.start()
    return copies


def grow(table_ref, v, factor, above, below):
    middle = table_ref.shape[1] // FINE // 2 - 1
    low_pair, high_pair = (below, above), (above, below)
    table_ref[v, middle * FINE : (middle + 1) * FINE, :] = above.astype(jnp.bfloat16)
    table_ref[v, (middle + 1) * FINE : (middle + 2) * FINE, :] = below.astype(jnp.bfloat16)
    for n in range(1, middle + 1):
        low_pair = (low_pair[1], factor * low_pair[1] - low_pair[0])
        high_pair = (high_pair[1], factor * high_pair[1] - high_pair[0])
        for at, value in ((middle - n, low_pair[1]), (middle + 1 + n, high_pair[1])):
            table_ref[v, at * FINE : (at + 1) * FINE, :] = value.astype(jnp.bfloat16)


def cosine(turns, period):
    rest = turns - period * jnp.floor(turns * (1.0 / period))
    angle = (jnp.abs(rest - period // 2) - period // 4) * (2.0 * math.pi / period)
    return angle * series(angle * angle, [(-1.0) ** n / math.factorial(2 * n + 1) for n in range(7)])


def fill_computed(table_ref, first, count):
    steps = table_ref.shape[1]
    period = 4 * (2 * steps + 1)
    scale = math.sqrt(HORIZON / steps) * 2.0 / math.sqrt(2 * steps + 1)
    middle = steps // FINE // 2 - 1
    assert (2 * (middle + 2) * FINE) * (2 * steps) < 2**24

    def odds(shape, axis, first):
        return (2 * (first + lax.broadcasted_iota(jnp.int32, shape, axis)) + 1).astype(jnp.float32)

    def strip(v, carry):
        cols = odds((FINE, LANES), 1, (first + v) * LANES)
        factor = jnp.broadcast_to(2.0 * cosine(2.0 * FINE * cols[:8, :], period)[:1, :], (FINE, LANES))
        above, below = (
            scale * cosine(odds((FINE, LANES), 0, (middle + n) * FINE) * cols, period) for n in range(2)
        )
        grow(table_ref, v, factor, above, below)
        return carry

    lax.fori_loop(0, count, strip, 0)


def series(x, coefficients):
    total = jnp.full_like(x, coefficients[-1])
    for coefficient in coefficients[-2::-1]:
        total = total * x + coefficient
    return total


def lag_values(hurst_all, strips, steps):
    shape = (strips, LANES)
    lag = lax.broadcasted_iota(jnp.int32, shape, 0) * LANES + lax.broadcasted_iota(jnp.int32, shape, 1)
    expo = hurst_all - 0.5
    safe = jnp.maximum(lag, 1).astype(jnp.float32)
    odd = 1.0 / (2.0 * safe - 1.0)
    exponent = -2.0 * (expo + 1.0) * odd * series(odd * odd, [1.0 / (2 * n + 1) for n in range(9)])
    near = -exponent * series(exponent, [1.0 / math.factorial(n + 1) for n in range(11)])
    inner = jnp.where(lag >= 2, jnp.where(exponent > -0.7, near, 1.0 - jnp.exp(exponent)), 1.0)
    log_b = ((expo + 1.0) * jnp.log(safe) + jnp.log(inner) - jnp.log(expo + 1.0)) / expo
    values = jnp.sqrt(2.0 * hurst_all) * jnp.exp(expo * (log_b + math.log(HORIZON / steps)))
    return jnp.where(lag >= 1, values, 0.0)


def spread_lags(lags, toeplitz_ref):
    strips = toeplitz_ref.shape[0] // LANES
    row = lax.broadcasted_iota(jnp.int32, (LANES, LANES), 0)
    col = lax.broadcasted_iota(jnp.int32, (LANES, LANES), 1)
    before = jnp.zeros((LANES, LANES), jnp.float32)
    per = BLOCK // LANES
    for e in range(1 - per, strips):
        if e < 0:
            tile = jnp.zeros((LANES, LANES), jnp.bfloat16)
        else:
            spread = jnp.broadcast_to(lags[e : e + 1, :], (LANES, LANES))
            rolled = pltpu.roll(spread, 0, 1, stride=1, stride_axis=0)
            tile = jnp.where(col >= row, rolled, before).astype(jnp.bfloat16)
            before = rolled
        for c in range(per):
            r = strips - per + c - e
            if 0 <= r < strips:
                toeplitz_ref[r * LANES : (r + 1) * LANES, c * LANES : (c + 1) * LANES] = tile


def packed(orth_hbm, forward_hbm, out_ref, table_ref, forward, sems):
    rows, width = orth_hbm.shape
    small, *others = fetch(sems, (forward_hbm, forward), (orth_hbm, out_ref.at[:rows]))
    fill_computed(table_ref, 0, table_ref.shape[0])
    small.wait()
    curve = 0.5 * jnp.log(forward[...])
    high = curve.astype(jnp.bfloat16).astype(jnp.float32)
    middle = (curve - high).astype(jnp.bfloat16).astype(jnp.float32)
    low = curve - high - middle
    row = lax.broadcasted_iota(jnp.int32, (EXTRA, width), 0)
    extra = jnp.where(row == 0, high, jnp.where(row == 1, middle, jnp.where(row == 2, low, 0.0)))
    out_ref[rows:, :] = extra.astype(jnp.bfloat16)
    for copy in others:
        copy.wait()


def prepare(
    hurst_ref, eta_ref, rho_ref, own_hbm, maturity_hbm, strike_hbm,
    table_ref, toeplitz_ref, power_ref, factor_ref, own_ref, maturity_ref, strike_ref, sems,
):
    strips = power_ref.shape[1] // LANES
    steps = table_ref.shape[1]
    copies = fetch(sems, (own_hbm, own_ref), (maturity_hbm, maturity_ref), (strike_hbm, strike_ref))
    hurst = jnp.full((strips, LANES), hurst_ref[0], jnp.float32)
    step = lax.broadcasted_iota(jnp.int32, hurst.shape, 0) * LANES + lax.broadcasted_iota(jnp.int32, hurst.shape, 1)
    times = step.astype(jnp.float32) * (HORIZON / steps)
    power = jnp.where(times > 0.0, jnp.exp(2.0 * hurst * jnp.log(times)), 0.0)
    for n in range(strips):
        power_ref[:, n * LANES : (n + 1) * LANES] = power[n : n + 1, :]
    rho = jnp.full(factor_ref.shape, rho_ref[0], jnp.float32)
    row = lax.broadcasted_iota(jnp.int32, factor_ref.shape, 0)
    orth_scale = jnp.sqrt(1.0 - rho * rho) * math.sqrt(HORIZON / steps)
    factor_ref[...] = jnp.where(row == 0, 0.5 * eta_ref[0], jnp.where(row == 1, rho, orth_scale))
    spread_lags(lag_values(hurst, strips, steps), toeplitz_ref)
    fill_computed(table_ref, strips * EARLY // 16, table_ref.shape[0])
    for copy in copies:
        copy.wait()


def complete(maturity_ref, strike_ref, table_ref, mask_ref, strikes_ref):
    strips = mask_ref.shape[0] // LANES
    late = table_ref.shape[0]
    strikes_ref[...] = 0.5 + strike_ref[...].astype(jnp.float32) / (STRIKES - 1)
    quotes = maturity_ref.shape[1]
    last = maturity_ref[...].astype(jnp.float32)
    place = lax.broadcasted_iota(jnp.int32, (LANES, quotes), 0).astype(jnp.float32).astype(jnp.bfloat16)
    one, none = jnp.ones((LANES, quotes), jnp.bfloat16), jnp.zeros((LANES, quotes), jnp.bfloat16)
    for n in range(strips):
        until = jnp.clip(last - n * LANES, -1.0, float(LANES)).astype(jnp.bfloat16)
        mask_ref[n * LANES : (n + 1) * LANES, :] = jnp.where(place <= jnp.broadcast_to(until, (LANES, quotes)), one, none)
    fill_computed(table_ref, strips - late, late)


def products(pieces, table_refs, first, block):
    per = BLOCK // LANES
    strips = [(ref, n) for ref in table_refs for n in range(ref.shape[0])][block * per : (block + 1) * per]
    total = None
    for r, piece_ref in pieces:
        width = piece_ref.shape[1]
        rows = pl.ds(pl.multiple_of((first ^ r) * width, LANES), width)
        columns = jnp.concatenate([ref[n, rows, :] for ref, n in strips], axis=1)
        product = jnp.dot(piece_ref[...], columns, preferred_element_type=jnp.float32)
        total = product if total is None else total + product
    return total


def driven(axis, pieces, *refs):
    piece_refs = refs[:pieces]
    *table_refs, dw_ref = refs[pieces:]
    me = lax.axis_index(axis)
    steps = dw_ref.shape[1]
    for n in range(steps // BLOCK):
        dw = products(list(enumerate(piece_refs)), table_refs, me, n)
        dw_ref[:, n * BLOCK : (n + 1) * BLOCK] = dw.astype(jnp.bfloat16)


def split(values):
    high = values.astype(jnp.bfloat16)
    return high, (values - high.astype(jnp.float32)).astype(jnp.bfloat16)


def increments(factor_ref, decay_power, orth_ref, volterra, dw, cols):
    rows = volterra.shape[0]
    half_eta, rho, orth_scale = (jnp.concatenate([factor_ref[n : n + 1, :]] * (BLOCK // LANES), axis=1) for n in range(3))
    extra = orth_ref[rows : rows + EXTRA, cols].astype(jnp.float32)
    curve = extra[0:1, :] + extra[1:2, :] + extra[2:3, :] - half_eta * half_eta * decay_power
    root = jnp.exp(half_eta * volterra + curve)
    noise = rho * dw.astype(jnp.float32) + orth_scale * orth_ref[:rows, cols].astype(jnp.float32)
    return root, noise


def fold(increment, entering, enters):
    folded = functools.reduce(lambda a, b: a + b, [increment[:, k * LANES : (k + 1) * LANES] for k in range(BLOCK // LANES)])
    return entering + jnp.where(enters, folded, 0.0)


def picks(halves, mask_ref, blocks, width):
    rows = halves.shape[0] // 2
    until = jnp.concatenate([mask_ref[pl.ds(pl.multiple_of(block * width, BLOCK), width), :] for block in blocks], axis=0)
    both = jnp.dot(halves[...], until, preferred_element_type=jnp.float32)
    return both[:rows, :] + both[rows:, :]


def moved(pieces, ready, axis, *refs):
    factor_ref, power_ref, dw_ref, toeplitz_ref, mask_ref = refs[:5]
    orth_refs = refs[5 : 5 + ready]
    own_ref, entering_ref, picked_ref, *rest_refs, volterra, halves = refs[5 + ready :]
    rows, steps = dw_ref.shape
    width = steps // pieces
    half_step = 0.5 * HORIZON / steps
    me = lax.axis_index(axis)
    for n in range(steps // BLOCK):
        depth = (n + 1) * BLOCK
        volterra[:, n * BLOCK : depth] = jnp.dot(
            dw_ref[:, :depth], toeplitz_ref[steps - depth :, :], preferred_element_type=jnp.float32
        )
    entering = jnp.zeros((rows, LANES), jnp.float32)
    for r in range(ready):
        block = me ^ r
        for n in range(width // BLOCK):
            cols = slice(n * BLOCK, (n + 1) * BLOCK)
            at = pl.ds(pl.multiple_of(block * width + n * BLOCK, BLOCK), BLOCK)
            root, noise = increments(factor_ref, power_ref[:, at], orth_refs[r], volterra[:, at], dw_ref[:, at], cols)
            increment = root * (noise - half_step * root)
            put = slice(r * width + n * BLOCK, r * width + (n + 1) * BLOCK)
            halves[:rows, put], halves[rows:, put] = split(increment)
            if r == 0:
                own_ref[:, cols] = increment
            else:
                entering = fold(increment, entering, block < me)
    picked = picks(halves, mask_ref, [me ^ r for r in range(ready)], width)
    for r, rest_ref in enumerate(rest_refs, ready):
        rest_ref[...] = volterra[:, pl.ds(pl.multiple_of((me ^ r) * width, BLOCK), width)]
    entering_ref[...] = entering
    picked_ref[...] = picked


def priced(pieces, ready, axis, *refs):
    rest = pieces - ready
    factor_ref, power_ref, dw_ref, mask_ref, strike_ref, before_ref, begun_ref = refs[:7]
    volterra_refs, orth_refs = refs[7 : 7 + rest], refs[7 + rest : 7 + 2 * rest]
    sums_ref, entering_ref, halves = refs[7 + 2 * rest :]
    rows, steps = dw_ref.shape
    width = steps // pieces
    half_step = 0.5 * HORIZON / steps
    me = lax.axis_index(axis)
    entering = before_ref[...]
    picked = begun_ref[...]
    for r in range(ready, pieces):
        block = me ^ r
        for n in range(width // BLOCK):
            cols = slice(n * BLOCK, (n + 1) * BLOCK)
            at = pl.ds(pl.multiple_of(block * width + n * BLOCK, BLOCK), BLOCK)
            root, noise = increments(
                factor_ref, power_ref[:, at], orth_refs[r - ready], volterra_refs[r - ready][:, cols], dw_ref[:, at], cols
            )
            increment = root * (noise - half_step * root)
            put = slice((r - ready) * width + n * BLOCK, (r - ready) * width + (n + 1) * BLOCK)
            halves[:rows, put], halves[rows:, put] = split(increment)
            entering = fold(increment, entering, block < me)
    if rest:
        picked = picked + picks(halves, mask_ref, [me ^ r for r in range(ready, pieces)], width)
    entering_ref[...] = entering
    payoff = jnp.maximum(jnp.exp(picked) - strike_ref[...], 0.0)
    sums_ref[...] = jnp.sum(payoff, axis=0, keepdims=True)


def summed(own_ref, entering_ref, out_ref):
    width = own_ref.shape[1]
    row = lax.broadcasted_iota(jnp.int32, (BLOCK, BLOCK), 0)
    col = lax.broadcasted_iota(jnp.int32, (BLOCK, BLOCK), 1)
    upper = jnp.where(row <= col, 1.0, 0.0).astype(jnp.bfloat16)
    carry = jnp.sum(entering_ref[...], axis=1, keepdims=True)
    for n in range(width // BLOCK):
        cols = slice(n * BLOCK, (n + 1) * BLOCK)
        hi, lo = split(own_ref[:, cols])
        total = carry + (
            jnp.dot(hi, upper, preferred_element_type=jnp.float32) + jnp.dot(lo, upper, preferred_element_type=jnp.float32)
        )
        out_ref[:, cols] = total
        carry = total[:, BLOCK - 1 :]


VMEM = pl.BlockSpec(memory_space=pltpu.VMEM)
SMEM = pl.BlockSpec(memory_space=pltpu.SMEM)
HBM = pl.BlockSpec(memory_space=pltpu.HBM)


def swap(held, axis, dists):
    pairs = lambda dist: [(n, n ^ dist) for n in range(lax.axis_size(axis))]
    for dist in dists:
        held = held | {r ^ dist: lax.ppermute(piece, axis, pairs(dist)) for r, piece in held.items()}
    return held


def total_over(value, axis):
    count = lax.axis_size(axis)
    if count & (count - 1):
        return lax.psum(value, axis)
    dist = 1
    while dist < count:
        value = value + lax.ppermute(value, axis, [(n, n ^ dist) for n in range(count)])
        dist *= 2
    return value


def stay(value):
    return pltpu.with_memory_space_constraint(value, pltpu.HBM)


def limit(mib):
    return pltpu.CompilerParams(vmem_limit_bytes=mib << 20)


def on_device(normals, orth_normals, forward_var, hurst, eta, rho, strike_index, maturity_index):
    rows, width = normals.shape
    pieces = lax.axis_size("tm")
    steps = width * pieces
    quotes = strike_index.shape[0]
    strips = steps // LANES
    forward_row, strike_row, maturity_row = (value.reshape(1, -1) for value in (forward_var, strike_index, maturity_index))

    dists = [pieces >> n for n in range(1, pieces.bit_length())]
    held = swap({0: normals}, "tm", dists[:1])

    early = strips * EARLY // 16
    orth, early_table = pl.pallas_call(
        packed,
        out_shape=(
            jax.ShapeDtypeStruct((rows + EXTRA, width), jnp.bfloat16),
            jax.ShapeDtypeStruct((early, steps, LANES), jnp.bfloat16),
        ),
        in_specs=[HBM] * 2,
        out_specs=(VMEM,) * 2,
        scratch_shapes=[pltpu.VMEM((1, width), jnp.float32), pltpu.SemaphoreType.DMA((2,))],
        compiler_params=limit(8),
        cost_estimate=pl.CostEstimate(flops=width, bytes_accessed=4 * rows * width, transcendentals=width),
        name="packed",
    )(stay(orth_normals), stay(forward_row))
    early_table, strike_row = lax.optimization_barrier((early_table, strike_row))
    orth_held = swap({0: orth}, "tm", dists[:1])

    middle = min(MIDDLE * strips // 16, strips - early)
    late = strips - early - middle
    middle_table, toeplitz, power, factors, own_weights, maturity_held, strike_held = pl.pallas_call(
        prepare,
        out_shape=(
            jax.ShapeDtypeStruct((middle, steps, LANES), jnp.bfloat16),
            jax.ShapeDtypeStruct((steps, BLOCK), jnp.bfloat16),
            jax.ShapeDtypeStruct((1, steps), jnp.float32),
            jax.ShapeDtypeStruct((8, LANES), jnp.float32),
            jax.ShapeDtypeStruct((rows, width), jnp.bfloat16),
            jax.ShapeDtypeStruct((1, quotes), jnp.int32),
            jax.ShapeDtypeStruct((1, quotes), jnp.int32),
        ),
        in_specs=[SMEM] * 3 + [HBM] * 3,
        out_specs=(VMEM,) * 7,
        scratch_shapes=[pltpu.SemaphoreType.DMA((3,))],
        compiler_params=limit(8),
        cost_estimate=pl.CostEstimate(flops=steps * steps, bytes_accessed=steps * steps, transcendentals=steps),
        name="prepare",
    )(hurst, eta, rho, *map(stay, (normals, maturity_row, strike_row)))

    far = {r: piece for r, piece in held.items() if r}
    far, maturity_held = lax.optimization_barrier((far, maturity_held))
    held = swap(held | far, "tm", dists[1:])
    weight_pieces = [own_weights] + [held[r] for r in range(1, pieces)]

    late_table, mask, strikes = pl.pallas_call(
        complete,
        out_shape=(
            jax.ShapeDtypeStruct((late, steps, LANES), jnp.bfloat16),
            jax.ShapeDtypeStruct((steps, quotes), jnp.bfloat16),
            jax.ShapeDtypeStruct((1, quotes), jnp.float32),
        ),
        in_specs=[VMEM] * 2,
        out_specs=(VMEM,) * 3,
        compiler_params=limit(8),
        cost_estimate=pl.CostEstimate(flops=steps, bytes_accessed=steps, transcendentals=0),
        name="complete",
    )(maturity_held, strike_held)

    dw = pl.pallas_call(
        functools.partial(driven, "tm", pieces),
        out_shape=jax.ShapeDtypeStruct((rows, steps), jnp.bfloat16),
        in_specs=[VMEM] * (pieces + 3),
        out_specs=VMEM,
        compiler_params=limit(8),
        cost_estimate=pl.CostEstimate(flops=steps, bytes_accessed=steps, transcendentals=0),
        name="driven",
    )(*weight_pieces, early_table, middle_table, late_table)

    far = {r: piece for r, piece in orth_held.items() if r}
    far, dw = lax.optimization_barrier((far, dw))
    orth_held = swap(orth_held | far, "tm", dists[1:])
    orth_pieces = [orth_held[r] for r in range(pieces)]
    ready = max(pieces - 1, 1)
    rest = pieces - ready

    own, entering, picked, *volterra = pl.pallas_call(
        functools.partial(moved, pieces, ready, "tm"),
        out_shape=(
            jax.ShapeDtypeStruct((rows, width), jnp.float32),
            jax.ShapeDtypeStruct((rows, LANES), jnp.float32),
            jax.ShapeDtypeStruct((rows, quotes), jnp.float32),
        )
        + (jax.ShapeDtypeStruct((rows, width), jnp.float32),) * rest,
        in_specs=[VMEM] * (5 + ready),
        out_specs=(VMEM,) * (3 + rest),
        scratch_shapes=[pltpu.VMEM((rows, steps), jnp.float32), pltpu.VMEM((2 * rows, ready * width), jnp.bfloat16)],
        compiler_params=limit(16),
        cost_estimate=pl.CostEstimate(flops=4 * rows * steps * quotes, bytes_accessed=8 * rows * steps, transcendentals=rows * steps),
        name="moved",
    )(factors, power, dw, toeplitz, mask, *orth_pieces[:ready])

    payoffs, entering = pl.pallas_call(
        functools.partial(priced, pieces, ready, "tm"),
        out_shape=(jax.ShapeDtypeStruct((1, quotes), jnp.float32), jax.ShapeDtypeStruct((rows, LANES), jnp.float32)),
        in_specs=[VMEM] * (7 + 2 * rest),
        out_specs=(VMEM,) * 2,
        scratch_shapes=[pltpu.VMEM((2 * rows, max(rest, 1) * width), jnp.bfloat16)],
        compiler_params=limit(8),
        cost_estimate=pl.CostEstimate(flops=rows * steps * quotes, bytes_accessed=2 * rows * steps, transcendentals=rows * width),
        name="priced",
    )(factors, power, dw, mask, strikes, entering, picked, *volterra, *orth_pieces[ready:])

    log_price = pl.pallas_call(
        summed,
        out_shape=jax.ShapeDtypeStruct((rows, width), jnp.float32),
        in_specs=[VMEM] * 2,
        out_specs=VMEM,
        compiler_params=limit(4),
        cost_estimate=pl.CostEstimate(flops=4 * rows * width * BLOCK, bytes_accessed=8 * rows * width, transcendentals=0),
        name="summed",
    )(own, entering)

    prices = total_over(payoffs, "path").reshape(quotes) / (rows * lax.axis_size("path"))
    return (log_price, prices)


def solution(mesh):
    in_specs = (
        P(("set", "path"), "tm"),
        P(("set", "path"), "tm"),
        P(("set", "tm")),
        P("set"),
        P("set"),
        P("set"),
        P("set"),
        P("set"),
    )
    out_specs = (P(("set", "path"), "tm"), P("set"))
    return jax.shard_map(on_device, mesh=mesh, in_specs=in_specs, out_specs=out_specs, check_vma=False)
```

```python
import functools
import math

import jax
import jax.numpy as jnp
from jax import lax
from jax.experimental import pallas as pl
from jax.experimental.pallas import tpu as pltpu
from jax.sharding import PartitionSpec as P

STRIKES = 11
HORIZON = 2.0
LANES = 128
BLOCK = 256
EXTRA = 8
FINE = 64
MIDDLE = 4
EARLY = 7


def fetch(sems, *pairs):
    copies = [pltpu.make_async_copy(source, target, sems.at[n]) for n, (source, target) in enumerate(pairs)]
    for copy in copies:
        copy.start()
    return copies


def grow(table_ref, v, factor, above, below):
    middle = table_ref.shape[1] // FINE // 2 - 1
    low_pair, high_pair = (below, above), (above, below)
    table_ref[v, middle * FINE : (middle + 1) * FINE, :] = above.astype(jnp.bfloat16)
    table_ref[v, (middle + 1) * FINE : (middle + 2) * FINE, :] = below.astype(jnp.bfloat16)
    for n in range(1, middle + 1):
        low_pair = (low_pair[1], factor * low_pair[1] - low_pair[0])
        high_pair = (high_pair[1], factor * high_pair[1] - high_pair[0])
        for at, value in ((middle - n, low_pair[1]), (middle + 1 + n, high_pair[1])):
            table_ref[v, at * FINE : (at + 1) * FINE, :] = value.astype(jnp.bfloat16)


def cosine(turns, period):
    rest = turns - period * jnp.floor(turns * (1.0 / period))
    angle = (jnp.abs(rest - period // 2) - period // 4) * (2.0 * math.pi / period)
    return angle * series(angle * angle, [(-1.0) ** n / math.factorial(2 * n + 1) for n in range(7)])


def fill_computed(table_ref, first, count):
    steps = table_ref.shape[1]
    period = 4 * (2 * steps + 1)
    scale = math.sqrt(HORIZON / steps) * 2.0 / math.sqrt(2 * steps + 1)
    middle = steps // FINE // 2 - 1
    assert (2 * (middle + 2) * FINE) * (2 * steps) < 2**24

    def odds(shape, axis, first):
        return (2 * (first + lax.broadcasted_iota(jnp.int32, shape, axis)) + 1).astype(jnp.float32)

    def strip(v, carry):
        cols = odds((FINE, LANES), 1, (first + v) * LANES)
        factor = jnp.broadcast_to(2.0 * cosine(2.0 * FINE * cols[:8, :], period)[:1, :], (FINE, LANES))
        above, below = (
            scale * cosine(odds((FINE, LANES), 0, (middle + n) * FINE) * cols, period) for n in range(2)
        )
        grow(table_ref, v, factor, above, below)
        return carry

    lax.fori_loop(0, count, strip, 0)


def series(x, coefficients):
    total = jnp.full_like(x, coefficients[-1])
    for coefficient in coefficients[-2::-1]:
        total = total * x + coefficient
    return total


def lag_values(hurst_all, strips, steps):
    shape = (strips, LANES)
    lag = lax.broadcasted_iota(jnp.int32, shape, 0) * LANES + lax.broadcasted_iota(jnp.int32, shape, 1)
    expo = hurst_all - 0.5
    safe = jnp.maximum(lag, 1).astype(jnp.float32)
    odd = 1.0 / (2.0 * safe - 1.0)
    exponent = -2.0 * (expo + 1.0) * odd * series(odd * odd, [1.0 / (2 * n + 1) for n in range(9)])
    near = -exponent * series(exponent, [1.0 / math.factorial(n + 1) for n in range(11)])
    inner = jnp.where(lag >= 2, jnp.where(exponent > -0.7, near, 1.0 - jnp.exp(exponent)), 1.0)
    log_b = ((expo + 1.0) * jnp.log(safe) + jnp.log(inner) - jnp.log(expo + 1.0)) / expo
    values = jnp.sqrt(2.0 * hurst_all) * jnp.exp(expo * (log_b + math.log(HORIZON / steps)))
    return jnp.where(lag >= 1, values, 0.0)


def spread_lags(lags, toeplitz_ref):
    strips = toeplitz_ref.shape[0] // LANES
    row = lax.broadcasted_iota(jnp.int32, (LANES, LANES), 0)
    col = lax.broadcasted_iota(jnp.int32, (LANES, LANES), 1)
    before = jnp.zeros((LANES, LANES), jnp.float32)
    per = BLOCK // LANES
    for e in range(1 - per, strips):
        if e < 0:
            tile = jnp.zeros((LANES, LANES), jnp.bfloat16)
        else:
            spread = jnp.broadcast_to(lags[e : e + 1, :], (LANES, LANES))
            rolled = pltpu.roll(spread, 0, 1, stride=1, stride_axis=0)
            tile = jnp.where(col >= row, rolled, before).astype(jnp.bfloat16)
            before = rolled
        for c in range(per):
            r = strips - per + c - e
            if 0 <= r < strips:
                toeplitz_ref[r * LANES : (r + 1) * LANES, c * LANES : (c + 1) * LANES] = tile


def packed(
    orth_hbm, forward_hbm, own_hbm, maturity_hbm, strike_hbm, out_ref, table_ref, own_ref, maturity_ref, strike_ref, forward, sems
):
    rows, width = orth_hbm.shape
    small, *others = fetch(
        sems, (forward_hbm, forward), (orth_hbm, out_ref.at[:rows]), (own_hbm, own_ref), (maturity_hbm, maturity_ref),
        (strike_hbm, strike_ref),
    )
    fill_computed(table_ref, 0, table_ref.shape[0])
    small.wait()
    curve = 0.5 * jnp.log(forward[...])
    high = curve.astype(jnp.bfloat16).astype(jnp.float32)
    middle = (curve - high).astype(jnp.bfloat16).astype(jnp.float32)
    low = curve - high - middle
    row = lax.broadcasted_iota(jnp.int32, (EXTRA, width), 0)
    extra = jnp.where(row == 0, high, jnp.where(row == 1, middle, jnp.where(row == 2, low, 0.0)))
    out_ref[rows:, :] = extra.astype(jnp.bfloat16)
    for copy in others:
        copy.wait()


def prepare(hurst_ref, eta_ref, rho_ref, maturity_ref, table_ref, toeplitz_ref, power_ref, factor_ref):
    strips = power_ref.shape[1] // LANES
    steps = table_ref.shape[1]
    hurst = jnp.full((strips, LANES), hurst_ref[0], jnp.float32)
    step = lax.broadcasted_iota(jnp.int32, hurst.shape, 0) * LANES + lax.broadcasted_iota(jnp.int32, hurst.shape, 1)
    times = step.astype(jnp.float32) * (HORIZON / steps)
    power = jnp.where(times > 0.0, jnp.exp(2.0 * hurst * jnp.log(times)), 0.0)
    for n in range(strips):
        power_ref[:, n * LANES : (n + 1) * LANES] = power[n : n + 1, :]
    rho = jnp.full(factor_ref.shape, rho_ref[0], jnp.float32)
    row = lax.broadcasted_iota(jnp.int32, factor_ref.shape, 0)
    orth_scale = jnp.sqrt(1.0 - rho * rho) * math.sqrt(HORIZON / steps)
    factor_ref[...] = jnp.where(row == 0, 0.5 * eta_ref[0], jnp.where(row == 1, rho, orth_scale))
    spread_lags(lag_values(hurst, strips, steps), toeplitz_ref)
    fill_computed(table_ref, strips * EARLY // 16, table_ref.shape[0])


def complete(maturity_ref, strike_ref, table_ref, mask_ref, strikes_ref):
    strips = mask_ref.shape[0] // LANES
    late = table_ref.shape[0]
    strikes_ref[...] = 0.5 + strike_ref[...].astype(jnp.float32) / (STRIKES - 1)
    quotes = maturity_ref.shape[1]
    last = maturity_ref[...].astype(jnp.float32)
    place = lax.broadcasted_iota(jnp.int32, (LANES, quotes), 0).astype(jnp.float32).astype(jnp.bfloat16)
    one, none = jnp.ones((LANES, quotes), jnp.bfloat16), jnp.zeros((LANES, quotes), jnp.bfloat16)
    for n in range(strips):
        until = jnp.clip(last - n * LANES, -1.0, float(LANES)).astype(jnp.bfloat16)
        mask_ref[n * LANES : (n + 1) * LANES, :] = jnp.where(place <= jnp.broadcast_to(until, (LANES, quotes)), one, none)
    fill_computed(table_ref, strips - late, late)


def products(pieces, table_refs, first, block):
    per = BLOCK // LANES
    strips = [(ref, n) for ref in table_refs for n in range(ref.shape[0])][block * per : (block + 1) * per]
    total = None
    for r, piece_ref in pieces:
        width = piece_ref.shape[1]
        rows = pl.ds(pl.multiple_of((first ^ r) * width, LANES), width)
        columns = jnp.concatenate([ref[n, rows, :] for ref, n in strips], axis=1)
        product = jnp.dot(piece_ref[...], columns, preferred_element_type=jnp.float32)
        total = product if total is None else total + product
    return total


def driven(axis, pieces, *refs):
    piece_refs = refs[:pieces]
    *table_refs, dw_ref = refs[pieces:]
    me = lax.axis_index(axis)
    steps = dw_ref.shape[1]
    for n in range(steps // BLOCK):
        dw = products(list(enumerate(piece_refs)), table_refs, me, n)
        dw_ref[:, n * BLOCK : (n + 1) * BLOCK] = dw.astype(jnp.bfloat16)


def split(values):
    high = values.astype(jnp.bfloat16)
    return high, (values - high.astype(jnp.float32)).astype(jnp.bfloat16)


def increments(factor_ref, decay_power, orth_ref, volterra, dw, cols):
    rows = volterra.shape[0]
    half_eta, rho, orth_scale = (jnp.concatenate([factor_ref[n : n + 1, :]] * (BLOCK // LANES), axis=1) for n in range(3))
    extra = orth_ref[rows : rows + EXTRA, cols].astype(jnp.float32)
    curve = extra[0:1, :] + extra[1:2, :] + extra[2:3, :] - half_eta * half_eta * decay_power
    root = jnp.exp(half_eta * volterra + curve)
    noise = rho * dw.astype(jnp.float32) + orth_scale * orth_ref[:rows, cols].astype(jnp.float32)
    return root, noise


def fold(increment, entering, enters):
    folded = functools.reduce(lambda a, b: a + b, [increment[:, k * LANES : (k + 1) * LANES] for k in range(BLOCK // LANES)])
    return entering + jnp.where(enters, folded, 0.0)


def picks(halves, mask_ref, blocks, width):
    rows = halves.shape[0] // 2
    until = jnp.concatenate([mask_ref[pl.ds(pl.multiple_of(block * width, BLOCK), width), :] for block in blocks], axis=0)
    both = jnp.dot(halves[...], until, preferred_element_type=jnp.float32)
    return both[:rows, :] + both[rows:, :]


def moved(pieces, ready, axis, *refs):
    factor_ref, power_ref, dw_ref, toeplitz_ref, mask_ref = refs[:5]
    orth_refs = refs[5 : 5 + ready]
    own_ref, entering_ref, picked_ref, *rest_refs, volterra, halves = refs[5 + ready :]
    rows, steps = dw_ref.shape
    width = steps // pieces
    half_step = 0.5 * HORIZON / steps
    me = lax.axis_index(axis)
    for n in range(steps // BLOCK):
        depth = (n + 1) * BLOCK
        volterra[:, n * BLOCK : depth] = jnp.dot(
            dw_ref[:, :depth], toeplitz_ref[steps - depth :, :], preferred_element_type=jnp.float32
        )
    entering = jnp.zeros((rows, LANES), jnp.float32)
    for r in range(ready):
        block = me ^ r
        for n in range(width // BLOCK):
            cols = slice(n * BLOCK, (n + 1) * BLOCK)
            at = pl.ds(pl.multiple_of(block * width + n * BLOCK, BLOCK), BLOCK)
            root, noise = increments(factor_ref, power_ref[:, at], orth_refs[r], volterra[:, at], dw_ref[:, at], cols)
            increment = root * (noise - half_step * root)
            put = slice(r * width + n * BLOCK, r * width + (n + 1) * BLOCK)
            halves[:rows, put], halves[rows:, put] = split(increment)
            if r == 0:
                own_ref[:, cols] = increment
            else:
                entering = fold(increment, entering, block < me)
    picked = picks(halves, mask_ref, [me ^ r for r in range(ready)], width)
    for r, rest_ref in enumerate(rest_refs, ready):
        rest_ref[...] = volterra[:, pl.ds(pl.multiple_of((me ^ r) * width, BLOCK), width)]
    entering_ref[...] = entering
    picked_ref[...] = picked


def priced(pieces, ready, axis, *refs):
    rest = pieces - ready
    factor_ref, power_ref, dw_ref, mask_ref, strike_ref, before_ref, begun_ref = refs[:7]
    volterra_refs, orth_refs = refs[7 : 7 + rest], refs[7 + rest : 7 + 2 * rest]
    sums_ref, entering_ref, halves = refs[7 + 2 * rest :]
    rows, steps = dw_ref.shape
    width = steps // pieces
    half_step = 0.5 * HORIZON / steps
    me = lax.axis_index(axis)
    entering = before_ref[...]
    picked = begun_ref[...]
    for r in range(ready, pieces):
        block = me ^ r
        for n in range(width // BLOCK):
            cols = slice(n * BLOCK, (n + 1) * BLOCK)
            at = pl.ds(pl.multiple_of(block * width + n * BLOCK, BLOCK), BLOCK)
            root, noise = increments(
                factor_ref, power_ref[:, at], orth_refs[r - ready], volterra_refs[r - ready][:, cols], dw_ref[:, at], cols
            )
            increment = root * (noise - half_step * root)
            put = slice((r - ready) * width + n * BLOCK, (r - ready) * width + (n + 1) * BLOCK)
            halves[:rows, put], halves[rows:, put] = split(increment)
            entering = fold(increment, entering, block < me)
    if rest:
        picked = picked + picks(halves, mask_ref, [me ^ r for r in range(ready, pieces)], width)
    entering_ref[...] = entering
    payoff = jnp.maximum(jnp.exp(picked) - strike_ref[...], 0.0)
    sums_ref[...] = jnp.sum(payoff, axis=0, keepdims=True)


def summed(own_ref, entering_ref, out_ref):
    width = own_ref.shape[1]
    row = lax.broadcasted_iota(jnp.int32, (BLOCK, BLOCK), 0)
    col = lax.broadcasted_iota(jnp.int32, (BLOCK, BLOCK), 1)
    upper = jnp.where(row <= col, 1.0, 0.0).astype(jnp.bfloat16)
    carry = jnp.sum(entering_ref[...], axis=1, keepdims=True)
    for n in range(width // BLOCK):
        cols = slice(n * BLOCK, (n + 1) * BLOCK)
        hi, lo = split(own_ref[:, cols])
        total = carry + (
            jnp.dot(hi, upper, preferred_element_type=jnp.float32) + jnp.dot(lo, upper, preferred_element_type=jnp.float32)
        )
        out_ref[:, cols] = total
        carry = total[:, BLOCK - 1 :]


VMEM = pl.BlockSpec(memory_space=pltpu.VMEM)
SMEM = pl.BlockSpec(memory_space=pltpu.SMEM)
HBM = pl.BlockSpec(memory_space=pltpu.HBM)


def swap(held, axis, dists):
    pairs = lambda dist: [(n, n ^ dist) for n in range(lax.axis_size(axis))]
    for dist in dists:
        held = held | {r ^ dist: lax.ppermute(piece, axis, pairs(dist)) for r, piece in held.items()}
    return held


def total_over(value, axis):
    count = lax.axis_size(axis)
    if count & (count - 1):
        return lax.psum(value, axis)
    dist = 1
    while dist < count:
        value = value + lax.ppermute(value, axis, [(n, n ^ dist) for n in range(count)])
        dist *= 2
    return value


def stay(value):
    return pltpu.with_memory_space_constraint(value, pltpu.HBM)


def limit(mib):
    return pltpu.CompilerParams(vmem_limit_bytes=mib << 20)


def on_device(normals, orth_normals, forward_var, hurst, eta, rho, strike_index, maturity_index):
    rows, width = normals.shape
    pieces = lax.axis_size("tm")
    steps = width * pieces
    quotes = strike_index.shape[0]
    strips = steps // LANES
    forward_row, strike_row, maturity_row = (value.reshape(1, -1) for value in (forward_var, strike_index, maturity_index))

    dists = [pieces >> n for n in range(1, pieces.bit_length())]
    held = swap({0: normals}, "tm", dists[:1])

    early = strips * EARLY // 16
    orth, early_table, own_weights, maturity_held, strike_held = pl.pallas_call(
        packed,
        out_shape=(
            jax.ShapeDtypeStruct((rows + EXTRA, width), jnp.bfloat16),
            jax.ShapeDtypeStruct((early, steps, LANES), jnp.bfloat16),
            jax.ShapeDtypeStruct((rows, width), jnp.bfloat16),
            jax.ShapeDtypeStruct((1, quotes), jnp.int32),
            jax.ShapeDtypeStruct((1, quotes), jnp.int32),
        ),
        in_specs=[HBM] * 5,
        out_specs=(VMEM,) * 5,
        scratch_shapes=[pltpu.VMEM((1, width), jnp.float32), pltpu.SemaphoreType.DMA((5,))],
        compiler_params=limit(8),
        cost_estimate=pl.CostEstimate(flops=width, bytes_accessed=4 * rows * width, transcendentals=width),
        name="packed",
    )(*map(stay, (orth_normals, forward_row, normals, maturity_row, strike_row)))
    orth_held = swap({0: orth}, "tm", dists[:1])

    middle = min(MIDDLE * strips // 16, strips - early)
    late = strips - early - middle
    middle_table, toeplitz, power, factors = pl.pallas_call(
        prepare,
        out_shape=(
            jax.ShapeDtypeStruct((middle, steps, LANES), jnp.bfloat16),
            jax.ShapeDtypeStruct((steps, BLOCK), jnp.bfloat16),
            jax.ShapeDtypeStruct((1, steps), jnp.float32),
            jax.ShapeDtypeStruct((8, LANES), jnp.float32),
        ),
        in_specs=[SMEM] * 3 + [VMEM],
        out_specs=(VMEM,) * 4,
        compiler_params=limit(8),
        cost_estimate=pl.CostEstimate(flops=steps * steps, bytes_accessed=steps * steps, transcendentals=steps),
        name="prepare",
    )(hurst, eta, rho, maturity_held)

    far = {r: piece for r, piece in held.items() if r}
    far, strike_held, power = lax.optimization_barrier((far, strike_held, power))
    held = swap(held | far, "tm", dists[1:])
    weight_pieces = [own_weights] + [held[r] for r in range(1, pieces)]

    late_table, mask, strikes = pl.pallas_call(
        complete,
        out_shape=(
            jax.ShapeDtypeStruct((late, steps, LANES), jnp.bfloat16),
            jax.ShapeDtypeStruct((steps, quotes), jnp.bfloat16),
            jax.ShapeDtypeStruct((1, quotes), jnp.float32),
        ),
        in_specs=[VMEM] * 2,
        out_specs=(VMEM,) * 3,
        compiler_params=limit(8),
        cost_estimate=pl.CostEstimate(flops=steps, bytes_accessed=steps, transcendentals=0),
        name="complete",
    )(maturity_held, strike_held)

    dw = pl.pallas_call(
        functools.partial(driven, "tm", pieces),
        out_shape=jax.ShapeDtypeStruct((rows, steps), jnp.bfloat16),
        in_specs=[VMEM] * (pieces + 3),
        out_specs=VMEM,
        compiler_params=limit(8),
        cost_estimate=pl.CostEstimate(flops=steps, bytes_accessed=steps, transcendentals=0),
        name="driven",
    )(*weight_pieces, early_table, middle_table, late_table)

    far = {r: piece for r, piece in orth_held.items() if r}
    far, dw = lax.optimization_barrier((far, dw))
    orth_held = swap(orth_held | far, "tm", dists[1:])
    orth_pieces = [orth_held[r] for r in range(pieces)]
    ready = max(pieces - 1, 1)
    rest = pieces - ready

    own, entering, picked, *volterra = pl.pallas_call(
        functools.partial(moved, pieces, ready, "tm"),
        out_shape=(
            jax.ShapeDtypeStruct((rows, width), jnp.float32),
            jax.ShapeDtypeStruct((rows, LANES), jnp.float32),
            jax.ShapeDtypeStruct((rows, quotes), jnp.float32),
        )
        + (jax.ShapeDtypeStruct((rows, width), jnp.float32),) * rest,
        in_specs=[VMEM] * (5 + ready),
        out_specs=(VMEM,) * (3 + rest),
        scratch_shapes=[pltpu.VMEM((rows, steps), jnp.float32), pltpu.VMEM((2 * rows, ready * width), jnp.bfloat16)],
        compiler_params=limit(16),
        cost_estimate=pl.CostEstimate(flops=4 * rows * steps * quotes, bytes_accessed=8 * rows * steps, transcendentals=rows * steps),
        name="moved",
    )(factors, power, dw, toeplitz, mask, *orth_pieces[:ready])

    payoffs, entering = pl.pallas_call(
        functools.partial(priced, pieces, ready, "tm"),
        out_shape=(jax.ShapeDtypeStruct((1, quotes), jnp.float32), jax.ShapeDtypeStruct((rows, LANES), jnp.float32)),
        in_specs=[VMEM] * (7 + 2 * rest),
        out_specs=(VMEM,) * 2,
        scratch_shapes=[pltpu.VMEM((2 * rows, max(rest, 1) * width), jnp.bfloat16)],
        compiler_params=limit(8),
        cost_estimate=pl.CostEstimate(flops=rows * steps * quotes, bytes_accessed=2 * rows * steps, transcendentals=rows * width),
        name="priced",
    )(factors, power, dw, mask, strikes, entering, picked, *volterra, *orth_pieces[ready:])

    log_price = pl.pallas_call(
        summed,
        out_shape=jax.ShapeDtypeStruct((rows, width), jnp.float32),
        in_specs=[VMEM] * 2,
        out_specs=VMEM,
        compiler_params=limit(4),
        cost_estimate=pl.CostEstimate(flops=4 * rows * width * BLOCK, bytes_accessed=8 * rows * width, transcendentals=0),
        name="summed",
    )(own, entering)

    prices = total_over(payoffs, "path").reshape(quotes) / (rows * lax.axis_size("path"))
    return (log_price, prices)


def solution(mesh):
    in_specs = (
        P(("set", "path"), "tm"),
        P(("set", "path"), "tm"),
        P(("set", "tm")),
        P("set"),
        P("set"),
        P("set"),
        P("set"),
        P("set"),
    )
    out_specs = (P(("set", "path"), "tm"), P("set"))
    return jax.shard_map(on_device, mesh=mesh, in_specs=in_specs, out_specs=out_specs, check_vma=False)
```

```python
import functools
import math

import jax
import jax.numpy as jnp
from jax import lax
from jax.experimental import pallas as pl
from jax.experimental.pallas import tpu as pltpu
from jax.sharding import PartitionSpec as P

STRIKES = 11
HORIZON = 2.0
LANES = 128
BLOCK = 256
EXTRA = 8
FINE = 64
MIDDLE = 4
EARLY = 7


def fetch(sems, *pairs):
    copies = [pltpu.make_async_copy(source, target, sems.at[n]) for n, (source, target) in enumerate(pairs)]
    for copy in copies:
        copy.start()
    return copies


def grow(table_ref, v, factor, above, below):
    middle = table_ref.shape[1] // FINE // 2 - 1
    low_pair, high_pair = (below, above), (above, below)
    table_ref[v, middle * FINE : (middle + 1) * FINE, :] = above.astype(jnp.bfloat16)
    table_ref[v, (middle + 1) * FINE : (middle + 2) * FINE, :] = below.astype(jnp.bfloat16)
    for n in range(1, middle + 1):
        low_pair = (low_pair[1], factor * low_pair[1] - low_pair[0])
        high_pair = (high_pair[1], factor * high_pair[1] - high_pair[0])
        for at, value in ((middle - n, low_pair[1]), (middle + 1 + n, high_pair[1])):
            table_ref[v, at * FINE : (at + 1) * FINE, :] = value.astype(jnp.bfloat16)


def cosine(turns, period):
    rest = turns - period * jnp.floor(turns * (1.0 / period))
    angle = (jnp.abs(rest - period // 2) - period // 4) * (2.0 * math.pi / period)
    return angle * series(angle * angle, [(-1.0) ** n / math.factorial(2 * n + 1) for n in range(7)])


def fill_computed(table_ref, first, count):
    steps = table_ref.shape[1]
    period = 4 * (2 * steps + 1)
    scale = math.sqrt(HORIZON / steps) * 2.0 / math.sqrt(2 * steps + 1)
    middle = steps // FINE // 2 - 1
    assert (2 * (middle + 2) * FINE) * (2 * steps) < 2**24

    def odds(shape, axis, first):
        return (2 * (first + lax.broadcasted_iota(jnp.int32, shape, axis)) + 1).astype(jnp.float32)

    def strip(v, carry):
        cols = odds((FINE, LANES), 1, (first + v) * LANES)
        factor = jnp.broadcast_to(2.0 * cosine(2.0 * FINE * cols[:8, :], period)[:1, :], (FINE, LANES))
        above, below = (
            scale * cosine(odds((FINE, LANES), 0, (middle + n) * FINE) * cols, period) for n in range(2)
        )
        grow(table_ref, v, factor, above, below)
        return carry

    lax.fori_loop(0, count, strip, 0)


def series(x, coefficients):
    total = jnp.full_like(x, coefficients[-1])
    for coefficient in coefficients[-2::-1]:
        total = total * x + coefficient
    return total


def lag_values(hurst_all, strips, steps):
    shape = (strips, LANES)
    lag = lax.broadcasted_iota(jnp.int32, shape, 0) * LANES + lax.broadcasted_iota(jnp.int32, shape, 1)
    expo = hurst_all - 0.5
    safe = jnp.maximum(lag, 1).astype(jnp.float32)
    odd = 1.0 / (2.0 * safe - 1.0)
    exponent = -2.0 * (expo + 1.0) * odd * series(odd * odd, [1.0 / (2 * n + 1) for n in range(9)])
    near = -exponent * series(exponent, [1.0 / math.factorial(n + 1) for n in range(11)])
    inner = jnp.where(lag >= 2, jnp.where(exponent > -0.7, near, 1.0 - jnp.exp(exponent)), 1.0)
    log_b = ((expo + 1.0) * jnp.log(safe) + jnp.log(inner) - jnp.log(expo + 1.0)) / expo
    values = jnp.sqrt(2.0 * hurst_all) * jnp.exp(expo * (log_b + math.log(HORIZON / steps)))
    return jnp.where(lag >= 1, values, 0.0)


def spread_lags(lags, toeplitz_ref):
    strips = toeplitz_ref.shape[0] // LANES
    row = lax.broadcasted_iota(jnp.int32, (LANES, LANES), 0)
    col = lax.broadcasted_iota(jnp.int32, (LANES, LANES), 1)
    before = jnp.zeros((LANES, LANES), jnp.float32)
    per = BLOCK // LANES
    for e in range(1 - per, strips):
        if e < 0:
            tile = jnp.zeros((LANES, LANES), jnp.bfloat16)
        else:
            spread = jnp.broadcast_to(lags[e : e + 1, :], (LANES, LANES))
            rolled = pltpu.roll(spread, 0, 1, stride=1, stride_axis=0)
            tile = jnp.where(col >= row, rolled, before).astype(jnp.bfloat16)
            before = rolled
        for c in range(per):
            r = strips - per + c - e
            if 0 <= r < strips:
                toeplitz_ref[r * LANES : (r + 1) * LANES, c * LANES : (c + 1) * LANES] = tile


def packed(
    orth_hbm, forward_hbm, own_hbm, maturity_hbm, strike_hbm, out_ref, table_ref, own_ref, maturity_ref, strike_ref, forward, sems
):
    rows, width = orth_hbm.shape
    small, *others = fetch(
        sems, (forward_hbm, forward), (orth_hbm, out_ref.at[:rows]), (own_hbm, own_ref), (maturity_hbm, maturity_ref),
        (strike_hbm, strike_ref),
    )
    fill_computed(table_ref, 0, table_ref.shape[0])
    small.wait()
    curve = 0.5 * jnp.log(forward[...])
    high = curve.astype(jnp.bfloat16).astype(jnp.float32)
    middle = (curve - high).astype(jnp.bfloat16).astype(jnp.float32)
    low = curve - high - middle
    row = lax.broadcasted_iota(jnp.int32, (EXTRA, width), 0)
    extra = jnp.where(row == 0, high, jnp.where(row == 1, middle, jnp.where(row == 2, low, 0.0)))
    out_ref[rows:, :] = extra.astype(jnp.bfloat16)
    for copy in others:
        copy.wait()


def prepare(hurst_ref, eta_ref, rho_ref, maturity_ref, table_ref, toeplitz_ref, power_ref, factor_ref):
    strips = power_ref.shape[1] // LANES
    steps = table_ref.shape[1]
    hurst = jnp.full((strips, LANES), hurst_ref[0], jnp.float32)
    step = lax.broadcasted_iota(jnp.int32, hurst.shape, 0) * LANES + lax.broadcasted_iota(jnp.int32, hurst.shape, 1)
    times = step.astype(jnp.float32) * (HORIZON / steps)
    power = jnp.where(times > 0.0, jnp.exp(2.0 * hurst * jnp.log(times)), 0.0)
    for n in range(strips):
        power_ref[:, n * LANES : (n + 1) * LANES] = power[n : n + 1, :]
    rho = jnp.full(factor_ref.shape, rho_ref[0], jnp.float32)
    row = lax.broadcasted_iota(jnp.int32, factor_ref.shape, 0)
    orth_scale = jnp.sqrt(1.0 - rho * rho) * math.sqrt(HORIZON / steps)
    factor_ref[...] = jnp.where(row == 0, 0.5 * eta_ref[0], jnp.where(row == 1, rho, orth_scale))
    spread_lags(lag_values(hurst, strips, steps), toeplitz_ref)
    fill_computed(table_ref, strips * EARLY // 16, table_ref.shape[0])


def complete(maturity_ref, strike_ref, table_ref, mask_ref, strikes_ref):
    strips = mask_ref.shape[0] // LANES
    late = table_ref.shape[0]
    strikes_ref[...] = 0.5 + strike_ref[...].astype(jnp.float32) / (STRIKES - 1)
    quotes = maturity_ref.shape[1]
    last = maturity_ref[...].astype(jnp.float32)
    place = lax.broadcasted_iota(jnp.int32, (LANES, quotes), 0).astype(jnp.float32).astype(jnp.bfloat16)
    one, none = jnp.ones((LANES, quotes), jnp.bfloat16), jnp.zeros((LANES, quotes), jnp.bfloat16)
    for n in range(strips):
        until = jnp.clip(last - n * LANES, -1.0, float(LANES)).astype(jnp.bfloat16)
        mask_ref[n * LANES : (n + 1) * LANES, :] = jnp.where(place <= jnp.broadcast_to(until, (LANES, quotes)), one, none)
    fill_computed(table_ref, strips - late, late)


def products(pieces, table_refs, first, block):
    per = BLOCK // LANES
    strips = [(ref, n) for ref in table_refs for n in range(ref.shape[0])][block * per : (block + 1) * per]
    total = None
    for r, piece_ref in pieces:
        width = piece_ref.shape[1]
        rows = pl.ds(pl.multiple_of((first ^ r) * width, LANES), width)
        columns = jnp.concatenate([ref[n, rows, :] for ref, n in strips], axis=1)
        product = jnp.dot(piece_ref[...], columns, preferred_element_type=jnp.float32)
        total = product if total is None else total + product
    return total


def driven(axis, pieces, *refs):
    piece_refs = refs[:pieces]
    *table_refs, dw_ref = refs[pieces:]
    me = lax.axis_index(axis)
    steps = dw_ref.shape[1]
    for n in range(steps // BLOCK):
        dw = products(list(enumerate(piece_refs)), table_refs, me, n)
        dw_ref[:, n * BLOCK : (n + 1) * BLOCK] = dw.astype(jnp.bfloat16)


def split(values):
    high = values.astype(jnp.bfloat16)
    return high, (values - high.astype(jnp.float32)).astype(jnp.bfloat16)


def increments(factor_ref, decay_power, orth_ref, volterra, dw, cols):
    rows = volterra.shape[0]
    half_eta, rho, orth_scale = (jnp.concatenate([factor_ref[n : n + 1, :]] * (BLOCK // LANES), axis=1) for n in range(3))
    extra = orth_ref[rows : rows + EXTRA, cols].astype(jnp.float32)
    curve = extra[0:1, :] + extra[1:2, :] + extra[2:3, :] - half_eta * half_eta * decay_power
    root = jnp.exp(half_eta * volterra + curve)
    noise = rho * dw.astype(jnp.float32) + orth_scale * orth_ref[:rows, cols].astype(jnp.float32)
    return root, noise


def fold(increment, entering, enters):
    folded = functools.reduce(lambda a, b: a + b, [increment[:, k * LANES : (k + 1) * LANES] for k in range(BLOCK // LANES)])
    return entering + jnp.where(enters, folded, 0.0)


def picks(halves, mask_ref, blocks, width):
    rows = halves.shape[0] // 2
    total = None
    for n, block in enumerate(blocks):
        until = mask_ref[pl.ds(pl.multiple_of(block * width, BLOCK), width), :]
        both = jnp.dot(halves[:, n * width : (n + 1) * width], until, preferred_element_type=jnp.float32)
        total = both if total is None else total + both
    return total[:rows, :] + total[rows:, :]


def moved(pieces, ready, axis, *refs):
    factor_ref, power_ref, dw_ref, toeplitz_ref, mask_ref = refs[:5]
    orth_refs = refs[5 : 5 + ready]
    picked_ref, halves, *rest_refs, volterra = refs[5 + ready :]
    rows, steps = dw_ref.shape
    width = steps // pieces
    half_step = 0.5 * HORIZON / steps
    me = lax.axis_index(axis)
    for n in range(steps // BLOCK):
        depth = (n + 1) * BLOCK
        volterra[:, n * BLOCK : depth] = jnp.dot(
            dw_ref[:, :depth], toeplitz_ref[steps - depth :, :], preferred_element_type=jnp.float32
        )
    for r in range(ready):
        block = me ^ r
        for n in range(width // BLOCK):
            cols = slice(n * BLOCK, (n + 1) * BLOCK)
            at = pl.ds(pl.multiple_of(block * width + n * BLOCK, BLOCK), BLOCK)
            root, noise = increments(factor_ref, power_ref[:, at], orth_refs[r], volterra[:, at], dw_ref[:, at], cols)
            increment = root * (noise - half_step * root)
            put = slice(r * width + n * BLOCK, r * width + (n + 1) * BLOCK)
            halves[:rows, put], halves[rows:, put] = split(increment)
    picked = picks(halves, mask_ref, [me ^ r for r in range(ready)], width)
    for r, rest_ref in enumerate(rest_refs, ready):
        rest_ref[...] = volterra[:, pl.ds(pl.multiple_of((me ^ r) * width, BLOCK), width)]
    picked_ref[...] = picked


def priced(pieces, ready, axis, *refs):
    rest = pieces - ready
    factor_ref, power_ref, dw_ref, mask_ref, strike_ref, begun_ref = refs[:6]
    volterra_refs, orth_refs = refs[6 : 6 + rest], refs[6 + rest : 6 + 2 * rest]
    sums_ref, halves = refs[6 + 2 * rest :]
    rows, steps = dw_ref.shape
    width = steps // pieces
    half_step = 0.5 * HORIZON / steps
    me = lax.axis_index(axis)
    picked = begun_ref[...]
    for r in range(ready, pieces):
        block = me ^ r
        for n in range(width // BLOCK):
            cols = slice(n * BLOCK, (n + 1) * BLOCK)
            at = pl.ds(pl.multiple_of(block * width + n * BLOCK, BLOCK), BLOCK)
            root, noise = increments(
                factor_ref, power_ref[:, at], orth_refs[r - ready], volterra_refs[r - ready][:, cols], dw_ref[:, at], cols
            )
            increment = root * (noise - half_step * root)
            put = slice((r - ready) * width + n * BLOCK, (r - ready) * width + (n + 1) * BLOCK)
            halves[:rows, put], halves[rows:, put] = split(increment)
    if rest:
        picked = picked + picks(halves, mask_ref, [me ^ r for r in range(ready, pieces)], width)
    payoff = jnp.maximum(jnp.exp(picked) - strike_ref[...], 0.0)
    sums_ref[...] = jnp.sum(payoff, axis=0, keepdims=True)


def summed(ready, axis, first_ref, last_ref, out_ref):
    rows, width = out_ref.shape
    me = lax.axis_index(axis)
    row = lax.broadcasted_iota(jnp.int32, (BLOCK, BLOCK), 0)
    col = lax.broadcasted_iota(jnp.int32, (BLOCK, BLOCK), 1)
    upper = jnp.where(row <= col, 1.0, 0.0).astype(jnp.bfloat16)
    entering = jnp.zeros((rows, LANES), jnp.float32)
    rest = lax.axis_size(axis) - ready
    for r in range(1, ready + rest):
        ref, at = (first_ref, r * width) if r < ready else (last_ref, (r - ready) * width)
        for n in range(width // BLOCK):
            cols = slice(at + n * BLOCK, at + (n + 1) * BLOCK)
            entering = fold(ref[:rows, cols].astype(jnp.float32) + ref[rows:, cols].astype(jnp.float32), entering, (me ^ r) < me)
    carry = jnp.sum(entering, axis=1, keepdims=True)
    for n in range(width // BLOCK):
        cols = slice(n * BLOCK, (n + 1) * BLOCK)
        both = jnp.dot(first_ref[:, cols], upper, preferred_element_type=jnp.float32)
        total = carry + (both[:rows, :] + both[rows:, :])
        out_ref[:, cols] = total
        carry = total[:, BLOCK - 1 :]


VMEM = pl.BlockSpec(memory_space=pltpu.VMEM)
SMEM = pl.BlockSpec(memory_space=pltpu.SMEM)
HBM = pl.BlockSpec(memory_space=pltpu.HBM)


def swap(held, axis, dists):
    pairs = lambda dist: [(n, n ^ dist) for n in range(lax.axis_size(axis))]
    for dist in dists:
        held = held | {r ^ dist: lax.ppermute(piece, axis, pairs(dist)) for r, piece in held.items()}
    return held


def total_over(value, axis):
    count = lax.axis_size(axis)
    if count & (count - 1):
        return lax.psum(value, axis)
    dist = 1
    while dist < count:
        value = value + lax.ppermute(value, axis, [(n, n ^ dist) for n in range(count)])
        dist *= 2
    return value


def stay(value):
    return pltpu.with_memory_space_constraint(value, pltpu.HBM)


def limit(mib):
    return pltpu.CompilerParams(vmem_limit_bytes=mib << 20)


def on_device(normals, orth_normals, forward_var, hurst, eta, rho, strike_index, maturity_index):
    rows, width = normals.shape
    pieces = lax.axis_size("tm")
    steps = width * pieces
    quotes = strike_index.shape[0]
    strips = steps // LANES
    forward_row, strike_row, maturity_row = (value.reshape(1, -1) for value in (forward_var, strike_index, maturity_index))

    dists = [pieces >> n for n in range(1, pieces.bit_length())]
    held = swap({0: normals}, "tm", dists[:1])

    early = strips * EARLY // 16
    orth, early_table, own_weights, maturity_held, strike_held = pl.pallas_call(
        packed,
        out_shape=(
            jax.ShapeDtypeStruct((rows + EXTRA, width), jnp.bfloat16),
            jax.ShapeDtypeStruct((early, steps, LANES), jnp.bfloat16),
            jax.ShapeDtypeStruct((rows, width), jnp.bfloat16),
            jax.ShapeDtypeStruct((1, quotes), jnp.int32),
            jax.ShapeDtypeStruct((1, quotes), jnp.int32),
        ),
        in_specs=[HBM] * 5,
        out_specs=(VMEM,) * 5,
        scratch_shapes=[pltpu.VMEM((1, width), jnp.float32), pltpu.SemaphoreType.DMA((5,))],
        compiler_params=limit(8),
        cost_estimate=pl.CostEstimate(flops=width, bytes_accessed=4 * rows * width, transcendentals=width),
        name="packed",
    )(*map(stay, (orth_normals, forward_row, normals, maturity_row, strike_row)))
    orth_held = swap({0: orth}, "tm", dists[:1])

    middle = min(MIDDLE * strips // 16, strips - early)
    late = strips - early - middle
    middle_table, toeplitz, power, factors = pl.pallas_call(
        prepare,
        out_shape=(
            jax.ShapeDtypeStruct((middle, steps, LANES), jnp.bfloat16),
            jax.ShapeDtypeStruct((steps, BLOCK), jnp.bfloat16),
            jax.ShapeDtypeStruct((1, steps), jnp.float32),
            jax.ShapeDtypeStruct((8, LANES), jnp.float32),
        ),
        in_specs=[SMEM] * 3 + [VMEM],
        out_specs=(VMEM,) * 4,
        compiler_params=limit(8),
        cost_estimate=pl.CostEstimate(flops=steps * steps, bytes_accessed=steps * steps, transcendentals=steps),
        name="prepare",
    )(hurst, eta, rho, maturity_held)

    far = {r: piece for r, piece in held.items() if r}
    far, strike_held, power = lax.optimization_barrier((far, strike_held, power))
    held = swap(held | far, "tm", dists[1:])
    weight_pieces = [own_weights] + [held[r] for r in range(1, pieces)]

    late_table, mask, strikes = pl.pallas_call(
        complete,
        out_shape=(
            jax.ShapeDtypeStruct((late, steps, LANES), jnp.bfloat16),
            jax.ShapeDtypeStruct((steps, quotes), jnp.bfloat16),
            jax.ShapeDtypeStruct((1, quotes), jnp.float32),
        ),
        in_specs=[VMEM] * 2,
        out_specs=(VMEM,) * 3,
        compiler_params=limit(8),
        cost_estimate=pl.CostEstimate(flops=steps, bytes_accessed=steps, transcendentals=0),
        name="complete",
    )(maturity_held, strike_held)

    dw = pl.pallas_call(
        functools.partial(driven, "tm", pieces),
        out_shape=jax.ShapeDtypeStruct((rows, steps), jnp.bfloat16),
        in_specs=[VMEM] * (pieces + 3),
        out_specs=VMEM,
        compiler_params=limit(8),
        cost_estimate=pl.CostEstimate(flops=steps, bytes_accessed=steps, transcendentals=0),
        name="driven",
    )(*weight_pieces, early_table, middle_table, late_table)

    far = {r: piece for r, piece in orth_held.items() if r}
    far, dw = lax.optimization_barrier((far, dw))
    orth_held = swap(orth_held | far, "tm", dists[1:])
    orth_pieces = [orth_held[r] for r in range(pieces)]
    ready = max(pieces - 1, 1)
    rest = pieces - ready

    picked, first_halves, *volterra = pl.pallas_call(
        functools.partial(moved, pieces, ready, "tm"),
        out_shape=(
            jax.ShapeDtypeStruct((rows, quotes), jnp.float32),
            jax.ShapeDtypeStruct((2 * rows, ready * width), jnp.bfloat16),
        )
        + (jax.ShapeDtypeStruct((rows, width), jnp.float32),) * rest,
        in_specs=[VMEM] * (5 + ready),
        out_specs=(VMEM,) * (2 + rest),
        scratch_shapes=[pltpu.VMEM((rows, steps), jnp.float32)],
        compiler_params=limit(16),
        cost_estimate=pl.CostEstimate(flops=4 * rows * steps * quotes, bytes_accessed=8 * rows * steps, transcendentals=rows * steps),
        name="moved",
    )(factors, power, dw, toeplitz, mask, *orth_pieces[:ready])

    payoffs, last_halves = pl.pallas_call(
        functools.partial(priced, pieces, ready, "tm"),
        out_shape=(
            jax.ShapeDtypeStruct((1, quotes), jnp.float32),
            jax.ShapeDtypeStruct((2 * rows, max(rest, 1) * width), jnp.bfloat16),
        ),
        in_specs=[VMEM] * (6 + 2 * rest),
        out_specs=(VMEM,) * 2,
        compiler_params=limit(8),
        cost_estimate=pl.CostEstimate(flops=rows * steps * quotes, bytes_accessed=2 * rows * steps, transcendentals=rows * width),
        name="priced",
    )(factors, power, dw, mask, strikes, picked, *volterra, *orth_pieces[ready:])

    log_price = pl.pallas_call(
        functools.partial(summed, ready, "tm"),
        out_shape=jax.ShapeDtypeStruct((rows, width), jnp.float32),
        in_specs=[VMEM] * 2,
        out_specs=VMEM,
        compiler_params=limit(4),
        cost_estimate=pl.CostEstimate(flops=4 * rows * width * BLOCK, bytes_accessed=8 * rows * width, transcendentals=0),
        name="summed",
    )(first_halves, last_halves)

    prices = total_over(payoffs, "path").reshape(quotes) / (rows * lax.axis_size("path"))
    return (log_price, prices)


def solution(mesh):
    in_specs = (
        P(("set", "path"), "tm"),
        P(("set", "path"), "tm"),
        P(("set", "tm")),
        P("set"),
        P("set"),
        P("set"),
        P("set"),
        P("set"),
    )
    out_specs = (P(("set", "path"), "tm"), P("set"))
    return jax.shard_map(on_device, mesh=mesh, in_specs=in_specs, out_specs=out_specs, check_vma=False)
```
